32 devices in a mesh: groups: 2 (over y), shard: 2 (over x), expert: 4 (over z), section: 2 (over core).
Axes of the slice: x: 2, y: 2, z: 4, core: 2. Of those that a mesh axis runs over, the one named last changes fastest.
Arguments:
- tokens: bfloat16 [2, 512, 6144], P(None, ('groups', 'shard', 'expert')), parts along dimension 1, may hold values from -6 to 6
- norm_gain: float32 [2, 6144], P('section'), may hold values from 0.5 to 2
- route_ids: int32 [2, 2, 512, 2], P('section', None, ('groups', 'shard', 'expert')), parts along dimension 2, may hold values from 0 to 3, all different within a row; in each aligned block of 32 rows (0 to 31, 32 to 63, ..., all dimensions but the last counted through in order) at most 18 rows name the same one
- route_weights: float32 [2, 2, 512, 2], P('section', None, ('groups', 'shard', 'expert')), parts along dimension 2, may hold values from 0.25 to 1
- gate_blocks: bfloat16 [2, 4, 64, 1, 128, 128], P('section', 'expert', 'shard'), may hold values from -0.5 to 0.5
- up_blocks: bfloat16 [2, 4, 64, 1, 128, 128], P('section', 'expert', 'shard'), may hold values from -0.5 to 0.5
- down_blocks: bfloat16 [2, 4, 64, 1, 128, 128], P('section', 'expert', 'shard'), may hold values from -0.4375 to 0.4375
- gate_rows: int32 [2, 4, 64, 1], P('section', 'expert', 'shard'), may hold values from 0 to 47
- down_cols: int32 [2, 4, 64, 1], P('section', 'expert', 'shard'), may hold values from 0 to 47
Outputs:
- hidden_states: bfloat16 [2, 2, 512, 6144], P('section', None, ('groups', 'shard', 'expert')), parts along dimension 2
The draws below stay inside these ranges and needn't reach their ends.
There are 2 independent parts, one for each index of `groups`. The reference program is written for one: setup_inputs(seed, part) draws one part's arguments, and reference() takes and returns one part's arrays. A program takes and returns all parts, laid end to end along the dimension named above; an argument that names none is the same for every part. Nothing has to cross between parts.
Inputs may be any that keep to these rules, and one draw needn't show every extreme that they name: `route_ids`: the 2 experts of a token differ; among the 32 tokens of one device, one micro-batch and one layer, no expert is named by more than 18 tokens, a bound that some block reaches of them.
All inputs are finite; a program needn't handle non-finite values.
Results may differ from the reference program's by a relative error of at most 0.0064.
Values may be sent and summed in bfloat16 or wider, within the bound.
A program may use at most 64 MiB of HBM per device.

```python
import math
import jax
import jax.numpy as jnp
import numpy as np
from jax import lax

D = 6144
FF = 8192
BLK = 128
KEEP = 1
TOP = 2
LAYERS = 2
MICRO = 2
TOK_MB = 32
EXPERTS = 4
CAP = 18
TOKENS = 256


def pick_blocks(key):
    block_rows = D // BLK
    scores = jax.random.randint(key, (LAYERS, EXPERTS, FF // BLK, block_rows), 0, 1 << 20, dtype=jnp.int32)
    scores = scores * block_rows + jnp.arange(block_rows, dtype=jnp.int32)
    return lax.top_k(scores, KEEP)[1].astype(jnp.int32)


def draw_gate_rows(key, part):
    return pick_blocks(jax.random.fold_in(key, 11))


def draw_down_cols(key, part):
    return pick_blocks(jax.random.fold_in(key, 23))


def block_scale(key, extent, pieces, smallest, high):
    factor_of, own = 1.0, jax.random.fold_in(key, 6)
    for position, shards_of in pieces:
        draws = jnp.exp(jax.random.uniform(jax.random.fold_in(own, position), (shards_of,), jnp.float32, smallest / len(pieces), high / len(pieces)))
        factor_of = factor_of * jnp.repeat(draws, extent[position] // shards_of).reshape([-1 if axis == position else 1 for axis in range(len(extent))])
    return factor_of


def assign_block(rng, own, number, rows, number_of, top, most, slope):
    order = jax.random.permutation(rng, number_of)
    packed, ordinary = load_shares(number_of, rows * top, most, slope, True), load_shares(number_of, rows * top, most, slope, False)
    places = jnp.arange(number_of)

    def named(lengths, offset_by):
        used = int((lengths > 0).sum())
        fixed = max(1, used // 4)
        shifted = fixed + (places - fixed + offset_by * (used - fixed)) % max(1, number_of - fixed)
        return jnp.zeros((number_of,), jnp.int32).at[order[jnp.where(places < fixed, places, shifted)]].set(jnp.asarray(lengths, jnp.int32))

    lengths = jnp.where(number % 4 == 0, named(packed, number // 4), named(ordinary, number - number // 4 - 1))
    mixed = jax.random.permutation(jax.random.fold_in(own, 3), number_of)
    donor, sink = mixed[0:number_of // 2 * 2:2], mixed[1:number_of // 2 * 2:2]
    room = jnp.minimum(lengths[donor] - 1, most - lengths[sink]) // 2
    room = jnp.where((donor == order[0]) | (sink == order[0]) | (lengths[sink] == 0), 0, jnp.maximum(room, 0))
    shifted = jax.random.randint(jax.random.fold_in(own, 4), (number_of // 2,), 0, 1 << 20) % (room + 1)
    lengths = lengths.at[donor].add(-shifted).at[sink].add(shifted)
    labels = jnp.searchsorted(jnp.cumsum(lengths), jnp.arange(rows * top), side="right").astype(jnp.int32)
    listing = labels.reshape(top, rows).T
    listing = listing[jax.random.permutation(jax.random.fold_in(own, 1), rows)]
    offset_by = jax.random.randint(jax.random.fold_in(own, 2), (rows, 1), 0, top)
    return jnp.take_along_axis(listing, (jnp.arange(top)[None, :] + offset_by) % top, axis=1)


def load_shares(count, total, reach, lean, full):
    weights = [(1 << 20) // math.isqrt(standing ** lean) + 1 for standing in range(1, count + 1)]
    largest = reach if full else min(reach, max(-(-total // count), total * weights[0] // sum(weights)))
    least = 1 if total - largest >= count - 1 else 0
    holding, rest = [largest] + [least] * (count - 1), total - largest - least * (count - 1)
    while rest > 0:
        free = [i for i in range(1, count) if holding[i] < largest] or [i for i in range(1, count) if holding[i] < reach]
        whole, remaining = sum([weights[i] for i in free]), rest
        for i in free:
            addition = min(reach - holding[i], max(1, remaining * weights[i] // whole), rest)
            holding[i] = holding[i] + addition
            rest = rest - addition
    return np.array(holding)


def gaussian(rng, shape, scale, most, pieces=(), held_as=jnp.bfloat16):
    array = jax.random.normal(rng, shape, jnp.float32) * scale
    if len(pieces) > 0:
        array = block_scale(rng, shape, pieces, -0.22, 0.18) * array
    return jnp.clip(array, min=-most, max=most).astype(held_as)


def setup_inputs(seed: int = 0, part: int = 0) -> dict:
    arg_keys = jax.random.split(jax.random.key(seed), 10)
    own_keys = jax.random.split(jax.random.fold_in(arg_keys[9], part), 10)
    tokens = gaussian(own_keys[0], (MICRO, TOKENS, D), 1.0, 6.0, ((1, 8),))
    norm_gain = jnp.clip(jnp.exp(math.log(2.0) - 1.3862944 * jax.random.uniform(arg_keys[1], (LAYERS, D), jnp.float32) ** block_scale(arg_keys[1], (LAYERS, D), ((0, 2),), -0.2, 0.2)), 0.5, 2.0)
    route_ids_keys = jax.random.split(jax.random.fold_in(own_keys[2], 1), LAYERS * MICRO * TOKENS // TOK_MB)
    route_ids_turns = jax.random.permutation(jax.random.fold_in(own_keys[2], 3), LAYERS * MICRO * TOKENS // TOK_MB)
    route_ids = jax.vmap(lambda own, number: assign_block(jax.random.fold_in(own_keys[2], 2), own, number, TOK_MB, EXPERTS, TOP, CAP, 2))(route_ids_keys, route_ids_turns).reshape((LAYERS, MICRO, TOKENS, TOP))
    route_weights = jnp.clip(0.25 + 0.75 * jax.random.uniform(own_keys[3], (LAYERS, MICRO, TOKENS, TOP), jnp.float32) ** block_scale(own_keys[3], (LAYERS, MICRO, TOKENS, TOP), ((0, 2), (2, 8)), -0.2, 0.2), 0.25, 1.0)
    gate_blocks = gaussian(arg_keys[4], (LAYERS, EXPERTS, FF // BLK, KEEP, BLK, BLK), (KEEP * BLK) ** -0.5, 0.5, ((0, 2), (1, 4), (2, 2)))
    up_blocks = gaussian(arg_keys[5], (LAYERS, EXPERTS, FF // BLK, KEEP, BLK, BLK), (KEEP * BLK) ** -0.5, 0.5, ((0, 2), (1, 4), (2, 2)))
    down_blocks = gaussian(arg_keys[6], (LAYERS, EXPERTS, FF // BLK, KEEP, BLK, BLK), (FF * KEEP * BLK // D) ** -0.5, 0.4375, ((0, 2), (1, 4), (2, 2)))
    gate_rows = draw_gate_rows(jax.random.fold_in(arg_keys[9], 71), part)
    down_cols = draw_down_cols(jax.random.fold_in(arg_keys[9], 71), part)
    return dict(tokens=tokens, norm_gain=norm_gain, route_ids=route_ids, route_weights=route_weights, gate_blocks=gate_blocks, up_blocks=up_blocks, down_blocks=down_blocks, gate_rows=gate_rows, down_cols=down_cols)


def normalize(values, gain_row):
    wide = values.astype(jnp.float32)
    scale = lax.rsqrt(lax.optimization_barrier(jnp.mean(wide * wide, axis=-1, keepdims=True)) + 1e-05)
    return (wide * scale * gain_row).astype(jnp.bfloat16)

def expert_rows(inputs, gate_w, up_w, down_w, row_index, col_index):
    row_total = inputs.shape[0]
    block_size = gate_w.shape[-1]
    block_rows = inputs.shape[1] // block_size
    blocks = inputs.reshape(row_total, block_rows, block_size)
    picked = jnp.take(blocks, row_index.reshape(-1), axis=1)
    picked = picked.reshape(row_total, row_index.shape[0], row_index.shape[1], block_size).astype(jnp.float32)
    gate = jnp.einsum('rckd,ckdf->rcf', picked, gate_w.astype(jnp.float32), precision=lax.Precision.HIGHEST)
    up_val = jnp.einsum('rckd,ckdf->rcf', picked, up_w.astype(jnp.float32), precision=lax.Precision.HIGHEST)
    hidden = (jax.nn.silu(gate) * up_val).astype(jnp.bfloat16).astype(jnp.float32)
    result = jnp.zeros((row_total, block_rows, block_size), jnp.float32)
    for kept in range(row_index.shape[1]):
        part_out = jnp.einsum('rcf,cfo->rco', hidden, down_w[:, kept].astype(jnp.float32), precision=lax.Precision.HIGHEST)
        result = result.at[:, col_index[:, kept].astype(jnp.int32)].add(part_out)
    return result.reshape(row_total, block_rows * block_size).astype(jnp.bfloat16)

def reference(tokens, norm_gain, route_ids, route_weights, gate_blocks, up_blocks, down_blocks, gate_rows, down_cols):
    limit = min(TOKENS, TOKENS // TOK_MB * CAP)
    state = tokens
    layer_outputs = []
    for layer in range(LAYERS):
        results = []
        for micro_index in range(MICRO):
            current = state[micro_index]
            normed = normalize(current, norm_gain[layer])
            chosen_ids = route_ids[layer, micro_index]
            chosen_weights = route_weights[layer, micro_index]
            total = current.astype(jnp.float32)
            for expert_index in range(EXPERTS):
                hits = chosen_ids == expert_index
                chosen = jnp.any(hits, axis=1)
                positions = jnp.nonzero(chosen, size=limit, fill_value=0)[0].astype(jnp.int32)
                valid = jnp.arange(limit, dtype=jnp.int32) < jnp.sum(chosen.astype(jnp.int32))
                weight_all = lax.optimization_barrier(jnp.sum(jnp.where(hits, chosen_weights, jnp.zeros((), chosen_weights.dtype)), axis=1))
                weight_rows = jnp.where(valid, weight_all[positions], jnp.zeros((), chosen_weights.dtype))
                produced = expert_rows(normed[positions], gate_blocks[layer, expert_index], up_blocks[layer, expert_index], down_blocks[layer, expert_index], gate_rows[layer, expert_index], down_cols[layer, expert_index])
                total = total.at[positions].add(weight_rows[:, None] * produced.astype(jnp.float32))
            results.append(total.astype(jnp.bfloat16))
        state = jnp.stack(results)
        layer_outputs.append(state)
    return jnp.stack(layer_outputs)
```

```python
import functools
import math

import jax
import jax.numpy as jnp
from jax import lax
from jax.experimental import pallas as pl
from jax.experimental.pallas import tpu as pltpu
from jax.sharding import PartitionSpec as P

TOP = 2
EPS = 1e-05
BF16 = jnp.bfloat16
F32 = jnp.float32
CUTS = 8


def layer_kernel(
    dims,
    tokens, gain, ids, mix, gate_hbm, up_hbm, down_hbm, rows_in, cols_in,
    out,
    held, disp, comb, comb_in, pieces, meta_here, normed, tails, send, recv, parts, ret_send, ret_recv,
    weights, meta_v, meta_s,
    tok_sem, hand_sem, own_sem, meta_own_sem, meta_send_sem, meta_recv_sem, meta_copy_sem, comb_sem,
    wx_send, wx_recv, wy_send, wy_recv, disp_send, disp_recv, disp_self,
    back_send, back_recv, back_self, go_sem,
):
    micro, rows, blocks, blk, cap, experts, shards, groups, sections, n_blk = dims
    main = cap // 16 * 16
    tail = cap - main
    tails_all = -(-(experts * tail) // 8) * 8
    slots = experts * main + tails_all
    folds = blocks // main
    tails_by = tails.reshape(blocks, tails_all, blk)
    me_g, me_s = lax.axis_index("groups"), lax.axis_index("shard")
    me_e, me_l = lax.axis_index("expert"), lax.axis_index("section")
    sizes = {"groups": groups, "shard": shards, "expert": experts, "section": sections}
    place = {"groups": me_g, "shard": me_s, "expert": me_e, "section": me_l}
    half = n_blk // groups
    cuts = math.gcd(half, CUTS)
    step = half // cuts
    sources = (gate_hbm, up_hbm, down_hbm)
    first, last = me_l == 0, me_l == sections - 1

    def remote(src, dst, ssem, rsem, device):
        return pltpu.make_async_remote_copy(
            src_ref=src, dst_ref=dst, send_sem=ssem, recv_sem=rsem,
            device_id=device, device_id_type=pl.DeviceIdType.MESH,
        )

    def peer(axis, by):
        return lax.rem(place[axis] + by, sizes[axis])

    def signal(sem, device):
        pl.semaphore_signal(sem, inc=1, device_id=device, device_id_type=pl.DeviceIdType.MESH)

    barrier = pltpu.get_barrier_semaphore()
    for by in range(experts - 1, 0, -1):
        signal(barrier, {"expert": peer("expert", by)})
        for hop in range(1, sections):
            signal(barrier, {"expert": peer("expert", by), "section": peer("section", hop)})
    for axis in ("groups", "shard", "section"):
        for by in range(1, sizes[axis]):
            signal(barrier, {axis: peer(axis, by)})
    greeted = sum(n - 1 for n in sizes.values()) + (experts - 1) * (sections - 1)

    def token_copy(m):
        return pltpu.make_async_copy(tokens.at[m], held.at[m], tok_sem.at[m])

    for m in range(micro):
        token_copy(m).start()
    own = [
        pltpu.make_async_copy(sources[a], weights.at[a, me_s], own_sem.at[a]) for a in range(3)
    ]
    for copy in own:
        copy.start()

    meta_own = pltpu.make_async_copy(meta_here, meta_v.at[me_s], meta_own_sem)

    def hand_back(m):
        return remote(
            held.at[m], out.at[m], hand_sem.at[0, m], hand_sem.at[1, m],
            {"section": peer("section", sections - 1)},
        )

    def comb_copy():
        return remote(
            comb, comb_in, comb_sem.at[0], comb_sem.at[1], {"section": peer("section", 1)}
        )

    def part(group, a, k, shard):
        return weights.at[a, shard, pl.ds(group * half + k * step, step)]

    def over_shard(a, k, by):
        i = k * 3 + a
        src = sources[a].at[pl.ds(me_g * half + k * step, step)]
        return remote(
            src, part(me_g, a, k, me_s), wx_send.at[i, by], wx_recv.at[i, by],
            {"shard": peer("shard", by)},
        )

    def over_groups(a, k, by, hop):
        i = k * 3 + a
        spot = part(me_g, a, k, peer("shard", shards - by))
        return remote(
            spot, spot, wy_send.at[i, by, hop], wy_recv.at[i, by, hop],
            {"groups": peer("groups", hop)},
        )

    def meta_over_shard(by):
        return remote(
            meta_here, meta_v.at[me_s], meta_send_sem.at[by], meta_recv_sem.at[by],
            {"shard": peer("shard", by)},
        )

    order = [(a, k, by) for k in range(cuts) for a in range(3) for by in range(1, shards)]

    def start_weights():
        for a, k, by in order:
            over_shard(a, k, by).start()

    def relay_weights(begin, end):
        for a, k, by in order:
            if begin <= k < end:
                over_shard(a, k, by).wait_recv()
                for hop in range(1, groups):
                    over_groups(a, k, by, hop).start()

    def finish_relay(at):
        for a, k, by in order:
            if k == at:
                for hop in range(1, groups):
                    over_groups(a, k, by, hop).wait()

    def partner(by):
        if experts & (experts - 1):
            return peer("expert", by)
        other, bit = me_e, 1
        while bit < experts:
            if by & bit:
                other = other + bit * (1 - 2 * lax.rem(me_e // bit, 2))
            bit *= 2
        return other

    def source(by):
        if experts & (experts - 1):
            return peer("expert", experts - by)
        return partner(by)

    far_first = sorted(range(1, experts), key=lambda by: (by < experts // 2, by))

    def chunk_out(m, by):
        return remote(
            send.at[m, partner(by)], recv[m].at[me_e], disp_send.at[m, by],
            disp_recv.at[m, by], {"expert": partner(by)},
        )

    def chunk_self(m):
        return pltpu.make_async_copy(send.at[m, me_e], recv[m].at[me_e], disp_self.at[m])

    def back_on(m, by):
        where = {"section": peer("section", 1)}
        if by > 0:
            where["expert"] = partner(by)
        return remote(
            ret_send.at[m, partner(by)], ret_recv.at[0, m, me_e], back_send.at[0, m, by],
            back_recv.at[0, m, by], where,
        )

    def back_home(m, by):
        return remote(
            ret_send.at[m, partner(by)], ret_recv.at[1, m, me_e], back_send.at[1, m, by],
            back_recv.at[1, m, by], {"expert": partner(by)},
        )

    def back_own(m):
        return pltpu.make_async_copy(
            ret_send.at[m, me_e], ret_recv.at[1, m, me_e], back_self.at[m]
        )

    def lanes(r):
        return pl.ds(pl.multiple_of(r * blk, blk), blk)

    def tail_line(e, j):
        return pl.ds(e * tail + j, blocks, stride=tails_all)

    def tail_part(j):
        return pl.ds(blocks + j * folds, folds)

    def put(dst, r, values):
        for e in range(experts):
            dst(e)[r] = values[e * main:(e + 1) * main].astype(BF16)
        tails_by[r] = values[experts * main:]

    def spread_tails(dst, e):
        for j in range(tail):
            lines = tails[tail_line(e, j), :].astype(BF16)
            dst(e)[tail_part(j)] = lines.reshape(folds, main, blk)

    def collect_tails(src):
        for e in range(experts):
            for j in range(tail):
                lines = src(e)[tail_part(j)].reshape(blocks, blk)
                tails[tail_line(e, j), :] = lines.astype(F32)

    def take(src, r):
        pieces_of = [src(e)[r] for e in range(experts)]
        return jnp.concatenate(pieces_of + [tails_by[r].astype(BF16)], axis=0)

    def dispatch(m):
        values = held[m].astype(F32)
        scale = lax.rsqrt(jnp.mean(values * values, axis=-1, keepdims=True) + EPS)
        normed[...] = (values * scale * gain[...]).astype(BF16)

        @pl.loop(0, blocks, unroll=8)
        def _(r):
            put(
                lambda e: send.at[m, e], r,
                jnp.dot(disp[m], normed[:, lanes(r)], preferred_element_type=F32),
            )

        for e in range(experts):
            spread_tails(lambda e: send.at[m, e], e)

    def send_chunks(m):
        for by in far_first:
            chunk_out(m, by).start()
        chunk_self(m).start()

    def segment(m, s, k):
        products = []
        for group in range(groups):
            for u in range(step):
                c = group * half + k * step + u
                at = (k * groups + group) * step + u
                x = take(lambda e: recv[m].at[e], meta_s[s, 0, c])
                gate = jnp.dot(x, weights[0, s, c], preferred_element_type=F32)
                up = jnp.dot(x, weights[1, s, c], preferred_element_type=F32)
                hidden = (gate / (1.0 + jnp.exp(-gate)) * up).astype(BF16)
                product = jnp.dot(hidden, weights[2, s, c], preferred_element_type=F32)
                products.append((at, c, product))
        for at, c, product in products:
            parts[s, at] = product + parts[s, meta_s[s, 1, c]]

    def expert_part(m, opening):
        chunk_self(m).wait()
        for by in far_first:
            chunk_out(m, by).wait()
        collect_tails(lambda e: recv[m].at[e])
        if opening:
            for copy in own:
                copy.wait()
            for by in range(1, shards):
                meta_over_shard(by).wait()
            meta_own.wait()
            load = pltpu.make_async_copy(meta_v, meta_s, meta_copy_sem)
            load.start()
            load.wait()
            for k in range(cuts):
                segment(m, me_s, k)
            for k in range(cuts):
                if early + k < cuts:
                    @pl.when(first)
                    def _():
                        relay_weights(early + k, early + k + 1)
                if early + k == cuts - 1:
                    @pl.when(first & (me_l < sections - 1))
                    def _():
                        signal(go_sem, {"section": peer("section", 1)})
                finish_relay(k)

                @pl.loop(1, shards)
                def _(by):
                    segment(m, peer("shard", shards - by), k)
            for a, k, by in order:
                over_shard(a, k, by).wait_send()
        else:
            @pl.loop(0, shards)
            def _(s):
                for k in range(cuts):
                    segment(m, s, k)

        @pl.loop(0, blocks, unroll=4)
        def _(j):
            total = parts[0, meta_s[0, 2, j]]
            for s in range(1, shards):
                total = total + parts[s, meta_s[s, 2, j]]
            put(lambda e: ret_send.at[m, e], j, total)

        for e in range(experts):
            spread_tails(lambda e: ret_send.at[m, e], e)

        @pl.when(me_l < sections - 1)
        def _():
            for by in far_first + [0]:
                back_on(m, by).start()

        @pl.when(last)
        def _():
            for by in far_first:
                back_home(m, by).start()
            back_own(m).start()

    def combine(m, which, dst):
        collect_tails(lambda e: ret_recv.at[which, m, e])

        @pl.loop(0, blocks, unroll=8)
        def _(r):
            mixed = jnp.dot(
                pieces[which, m], take(lambda e: ret_recv.at[which, m, e], r),
                preferred_element_type=F32,
            )
            mixed = mixed[:rows] + mixed[rows:2 * rows] + mixed[2 * rows:]
            dst[m, :, lanes(r)] = (held[m, :, lanes(r)].astype(F32) + mixed).astype(BF16)

    def split(which, m, value):
        for i in range(3):
            piece = value.astype(BF16)
            pieces[which, m, i * rows:(i + 1) * rows, :] = piece
            value = value - piece.astype(F32)

    def arrival(c):
        group = sum((c >= g * half).astype(jnp.int32) for g in range(1, groups))
        within = c - group * half
        k = sum((within >= i * step).astype(jnp.int32) for i in range(1, cuts))
        return k * (groups - 1) * step + group * step + within

    def iota(shape, axis):
        return lax.broadcasted_iota(jnp.int32, shape, axis)

    slot = iota((slots, rows), 0)
    inner = slot - experts * main
    head = inner < 0
    expert_main = sum((slot >= e * main).astype(jnp.int32) for e in range(1, experts))
    expert_tail = sum((inner >= e * tail).astype(jnp.int32) for e in range(1, experts + 1))
    expert = jnp.where(head, expert_main, expert_tail)
    place_in = jnp.where(head, slot - expert_main * main, main + inner - expert_tail * tail)
    place_in = place_in.astype(F32)
    earlier = (iota((rows, rows), 0) < iota((rows, rows), 1)).astype(F32).astype(BF16)
    for m in range(micro):
        named = [ids[m, j:j + 1, :] == expert for j in range(TOP)]
        hit = functools.reduce(jnp.logical_or, named)
        ahead = jnp.dot(
            hit.astype(F32).astype(BF16), earlier, preferred_element_type=F32
        )
        fits = hit & (ahead == place_in)
        amount = sum(jnp.where(named[j], mix[m, j:j + 1, :], 0.0) for j in range(TOP))
        disp[m] = fits.astype(F32).astype(BF16)
        comb[m] = jnp.transpose(jnp.where(fits, amount, 0.0))

    cols = cols_in[...]
    cols_down = jnp.transpose(jnp.broadcast_to(cols, (n_blk, n_blk)))
    from_place = arrival(iota((n_blk, n_blk), 0))
    chained = (cols_down == cols) & (from_place < arrival(iota((n_blk, n_blk), 1)))
    before = jnp.max(jnp.where(chained, from_place, -1), axis=0, keepdims=True)
    final = jnp.broadcast_to(cols_down[:, :1], (n_blk, blocks)) == iota((n_blk, blocks), 1)
    last_at = jnp.where(final, arrival(iota((n_blk, blocks), 0)), -1)
    last_at = jnp.max(last_at, axis=0, keepdims=True)
    meta_here[...] = jnp.zeros_like(meta_here)
    meta_here[0:1, 0:n_blk] = rows_in[...]
    meta_here[1:2, 0:n_blk] = jnp.where(before < 0, n_blk, before)
    meta_here[2:3, 0:blocks] = jnp.where(last_at < 0, n_blk, last_at)
    for s in range(shards):
        parts[s, n_blk] = jnp.zeros_like(parts[s, n_blk])
    early = cuts * 5 // 8

    for m in range(micro):
        token_copy(m).wait()

    @pl.when(first)
    def _():
        dispatch(0)

    @pl.when(last)
    def _():
        for m in range(micro):
            split(1, m, comb[m])

    pl.semaphore_wait(barrier, greeted)

    for by in range(1, shards):
        meta_over_shard(by).start()
    meta_own.start()

    @pl.when(first)
    def _():
        send_chunks(0)
        start_weights()

    @pl.when(me_l < sections - 1)
    def _():
        comb_copy().start()

    @pl.when(first)
    def _():
        for m in range(1, micro):
            dispatch(m)
            send_chunks(m)
        relay_weights(0, early)

    @pl.when(me_l > 0)
    def _():
        comb_copy().wait_recv()
        for m in range(micro):
            split(0, m, comb_in[m])
        pl.semaphore_wait(go_sem, 1)
        start_weights()
        for m in range(micro):
            if m == 0:
                relay_weights(0, cuts if micro == 1 else cuts - 1)
            if m == 1:
                relay_weights(cuts - 1, cuts)
            for by in far_first + [0]:
                back_on(m, by).wait_recv()
            combine(m, 0, held)
            hand_back(m).start()
            dispatch(m)
            send_chunks(m)

    for m in range(micro):
        expert_part(m, m == 0)

    @pl.when(last)
    def _():
        for m in range(micro):
            back_own(m).wait()
            for by in far_first:
                back_home(m, by).wait()
            combine(m, 1, out)

    @pl.when(me_l > 0)
    def _():
        for m in range(micro):
            hand_back(m).wait_send()

    @pl.when(me_l < sections - 1)
    def _():
        comb_copy().wait_send()
        for m in range(micro):
            for by in far_first + [0]:
                back_on(m, by).wait_send()
            hand_back(m).wait_recv()


def body(
    sizes,
    tokens,
    norm_gain,
    route_ids,
    route_weights,
    gate_blocks,
    up_blocks,
    down_blocks,
    gate_rows,
    down_cols,
):
    groups, shards, experts, sections = sizes
    assert sections == 2
    micro, rows, width = tokens.shape
    n_blk, blk = gate_blocks.shape[2], gate_blocks.shape[-1]
    blocks = width // blk
    cap = min(rows, max(rows * 9 // 16, rows * TOP // experts + 2))
    main = cap // 16 * 16
    tails_all = -(-(experts * (cap - main)) // 8) * 8
    slots = experts * main + tails_all

    cuts = math.gcd(n_blk // groups, CUTS)
    meta_width = -(-max(n_blk, blocks) // 128) * 128
    pieces = 3 * cuts
    dims = (micro, rows, blocks, blk, cap, experts, shards, groups, sections, n_blk)
    dma = pltpu.SemaphoreType.DMA
    assert blocks % main == 0
    chunk = (micro, experts, cap * blocks // main, main, blk)
    vmem, anywhere = pl.BlockSpec(memory_space=pltpu.VMEM), pl.BlockSpec(memory_space=pltpu.HBM)
    out = pl.pallas_call(
        functools.partial(layer_kernel, dims),
        out_shape=pltpu.VMEM((micro, rows, width), BF16),
        in_specs=[anywhere] + [vmem] * 3 + [anywhere] * 3 + [vmem] * 2,
        out_specs=vmem,
        scratch_shapes=[
            pltpu.VMEM((micro, rows, width), BF16),
            pltpu.VMEM((micro, slots, rows), BF16),
            pltpu.VMEM((micro, rows, slots), F32),
            pltpu.VMEM((micro, rows, slots), F32),
            pltpu.VMEM((2, micro, 3 * rows, slots), BF16),
            pltpu.VMEM((8, meta_width), jnp.int32),
            pltpu.VMEM((rows, width), BF16),
            pltpu.VMEM((tails_all * blocks, blk), F32),
            pltpu.VMEM(chunk, BF16),
            [pltpu.VMEM(chunk[1:], BF16) for _ in range(micro)],
            pltpu.VMEM((shards, n_blk + 1, slots, blk), F32),
            pltpu.VMEM(chunk, BF16),
            pltpu.VMEM((2,) + chunk, BF16),
            pltpu.VMEM((3, shards, n_blk, blk, blk), BF16),
            pltpu.VMEM((shards, 8, meta_width), jnp.int32),
            pltpu.SMEM((shards, 8, meta_width), jnp.int32),
            dma((micro,)),
            dma((2, micro)),
            dma((3,)),
            dma,
            dma((shards,)),
            dma((shards,)),
            dma,
            dma((2,)),
            dma((pieces, shards)),
            dma((pieces, shards)),
            dma((pieces, shards, groups)),
            dma((pieces, shards, groups)),
            dma((micro, experts)),
            dma((micro, experts)),
            dma((micro,)),
            dma((2, micro, experts)),
            dma((2, micro, experts)),
            dma((micro,)),
            pltpu.SemaphoreType.REGULAR,
        ],
        compiler_params=pltpu.CompilerParams(
            collective_id=0, has_side_effects=True, vmem_limit_bytes=56 * 1024 * 1024
        ),
    )(
        tokens, norm_gain, jnp.swapaxes(route_ids[0], 1, 2), jnp.swapaxes(route_weights[0], 1, 2),
        gate_blocks.reshape(n_blk, blk, blk), up_blocks.reshape(n_blk, blk, blk),
        down_blocks.reshape(n_blk, blk, blk), gate_rows.reshape(1, n_blk),
        down_cols.reshape(1, n_blk),
    )
    return out[None]


def solution(mesh):
    sizes = tuple(mesh.shape[name] for name in ("groups", "shard", "expert", "section"))
    in_specs = (
        P(None, ("groups", "shard", "expert"), None),
        P("section", None),
        P("section", None, ("groups", "shard", "expert"), None),
        P("section", None, ("groups", "shard", "expert"), None),
        P("section", "expert", "shard", None, None, None),
        P("section", "expert", "shard", None, None, None),
        P("section", "expert", "shard", None, None, None),
        P("section", "expert", "shard", None),
        P("section", "expert", "shard", None),
    )
    out_specs = P("section", None, ("groups", "shard", "expert"), None)
    return jax.shard_map(
        functools.partial(body, sizes), mesh=mesh, in_specs=in_specs, out_specs=out_specs,
        check_vma=False,
    )
```

```python
import functools
import math

import jax
import jax.numpy as jnp
from jax import lax
from jax.experimental import pallas as pl
from jax.experimental.pallas import tpu as pltpu
from jax.sharding import PartitionSpec as P

TOP = 2
EPS = 1e-05
BF16 = jnp.bfloat16
F32 = jnp.float32


def cut_list(half):
    cuts, at = [], 0
    while at < half:
        size = min(4, max(1, (half - at) // 2))
        cuts.append((at, size))
        at += size
    return cuts


def layer_kernel(
    dims,
    tokens, gain, ids, mix, gate_hbm, up_hbm, down_hbm, rows_in, cols_in,
    out,
    held, disp, comb, comb_in, pieces, meta_here, normed, tails, send, recv, parts, ret_send, ret_recv,
    weights, stage, meta_v, meta_s,
    tok_sem, hand_sem, own_sem, meta_own_sem, meta_send_sem, meta_recv_sem, meta_copy_sem, comb_sem,
    wx_send, wx_recv, wy_send, wy_recv, disp_send, disp_recv, disp_self,
    back_send, back_recv, back_self, sx_send, sx_recv, sc_send, sc_recv, sy_send, sy_recv,
):
    micro, rows, blocks, blk, cap, experts, shards, groups, sections, n_blk = dims
    main = cap // 16 * 16
    tail = cap - main
    tails_all = -(-(experts * tail) // 8) * 8
    slots = experts * main + tails_all
    folds = blocks // main
    tails_by = tails.reshape(blocks, tails_all, blk)
    me_g, me_s = lax.axis_index("groups"), lax.axis_index("shard")
    me_e, me_l = lax.axis_index("expert"), lax.axis_index("section")
    sizes = {"groups": groups, "shard": shards, "expert": experts, "section": sections}
    place = {"groups": me_g, "shard": me_s, "expert": me_e, "section": me_l}
    half = n_blk // groups
    cuts = cut_list(half)
    sources = (gate_hbm, up_hbm, down_hbm)
    first, last = me_l == 0, me_l == sections - 1

    def remote(src, dst, ssem, rsem, device):
        return pltpu.make_async_remote_copy(
            src_ref=src, dst_ref=dst, send_sem=ssem, recv_sem=rsem,
            device_id=device, device_id_type=pl.DeviceIdType.MESH,
        )

    def peer(axis, by):
        return lax.rem(place[axis] + by, sizes[axis])

    def signal(sem, device):
        pl.semaphore_signal(sem, inc=1, device_id=device, device_id_type=pl.DeviceIdType.MESH)

    barrier = pltpu.get_barrier_semaphore()
    for axis in ("expert", "shard", "groups"):
        for by in range(sizes[axis] - 1, 0, -1):
            for hop in range(sections):
                signal(barrier, {axis: peer(axis, by), "section": peer("section", hop)})
    for hop in range(1, sections):
        signal(barrier, {"section": peer("section", hop)})
    greeted = sections * (groups + shards + experts - 2) - 1

    def token_copy(m):
        return pltpu.make_async_copy(tokens.at[m], held.at[m], tok_sem.at[m])

    for m in range(micro):
        token_copy(m).start()
    for a in range(3):
        pltpu.make_async_copy(sources[a], weights.at[a, me_s], own_sem).start()

    meta_own = pltpu.make_async_copy(meta_here, meta_v.at[me_s], meta_own_sem)

    def hand_back(m):
        return remote(
            held.at[m], out.at[m], hand_sem.at[0, m], hand_sem.at[1, m],
            {"section": peer("section", sections - 1)},
        )

    def comb_copy():
        return remote(
            comb, comb_in, comb_sem.at[0], comb_sem.at[1], {"section": peer("section", 1)}
        )

    def spot(group, k, shard):
        return weights.at[:, shard, pl.ds(group * half + cuts[k][0], cuts[k][1])]

    def staged(k, shard):
        return stage.at[:, shard, pl.ds(*cuts[k])]

    def origin(by):
        return peer("shard", shards - by)

    def own_part(a, k):
        return sources[a].at[pl.ds(me_g * half + cuts[k][0], cuts[k][1])]

    pairs = [(k, by) for k in range(len(cuts)) for by in range(1, shards)]
    others = stage.at[:, pl.ds(0, shards - 1)]

    def start_stage():
        for k, by in pairs:
            for a in range(3):
                remote(
                    own_part(a, k), stage.at[a, me_s, pl.ds(*cuts[k])], sx_send,
                    sx_recv.at[k, by - 1],
                    {"shard": peer("shard", by), "section": peer("section", 1)},
                ).start()

    def stage_in(k, by):
        at = staged(k, origin(by))
        return remote(at, at, sx_send, sx_recv.at[k, by - 1], {"section": peer("section", 1)})

    def stage_down(k, by):
        return remote(
            staged(k, origin(by)), spot(me_g, k, origin(by)), sc_send, sc_recv.at[k, by - 1],
            {"section": peer("section", 1)},
        )

    def stage_over(k, by, hop, from_g):
        return remote(
            staged(k, origin(by)), spot(from_g, k, origin(by)), sy_send.at[hop - 1],
            sy_recv.at[k, by - 1, hop - 1],
            {"groups": peer("groups", hop), "section": peer("section", 1)},
        )

    def start_weights():
        for k, by in pairs:
            for a in range(3):
                remote(
                    own_part(a, k),
                    weights.at[a, me_s, pl.ds(me_g * half + cuts[k][0], cuts[k][1])],
                    wx_send, wx_recv.at[k, by - 1], {"shard": peer("shard", by)},
                ).start()

    def weights_in(k, by):
        at = spot(me_g, k, origin(by))
        return remote(at, at, wx_send, wx_recv.at[k, by - 1], {"shard": peer("shard", by)})

    def weights_over(k, by, hop, from_g):
        at = spot(from_g, k, origin(by))
        return remote(
            at, at, wy_send.at[hop - 1], wy_recv.at[k, by - 1, hop - 1],
            {"groups": peer("groups", hop)},
        )

    def all_sent(sem):
        remote(others, others, sem, wx_recv.at[0, 0], {"shard": peer("shard", 1)}).wait_send()

    def meta_over_shard(by):
        return remote(
            meta_here, meta_v.at[me_s], meta_send_sem.at[by - 1], meta_recv_sem.at[by - 1],
            {"shard": peer("shard", by)},
        )

    def relay_weights(begin, end):
        for k, by in pairs:
            if begin <= k < end:
                weights_in(k, by).wait_recv()
                for hop in range(1, groups):
                    weights_over(k, by, hop, me_g).start()

    def finish_relay(at):
        for k, by in pairs:
            if k == at:
                for hop in range(1, groups):
                    weights_over(k, by, hop, peer("groups", groups - hop)).wait_recv()

    def finish_stage(at):
        for k, by in pairs:
            if k == at:
                stage_down(k, by).wait_recv()
                for hop in range(1, groups):
                    stage_over(k, by, hop, peer("groups", groups - hop)).wait_recv()

    far_first = sorted(range(1, experts), key=lambda by: abs(by - experts // 2))

    def chunk_out(m, by):
        e = peer("expert", by)
        return remote(
            send.at[m, e], recv[m].at[me_e], disp_send.at[m], disp_recv.at[m], {"expert": e}
        )

    def chunk_self(m):
        return pltpu.make_async_copy(send.at[m, me_e], recv[m].at[me_e], disp_self.at[m])

    def chunks_far(m):
        return remote(
            send.at[m, pl.ds(0, experts - 1)], recv[m].at[pl.ds(0, experts - 1)],
            disp_send.at[m], disp_recv.at[m], {"expert": peer("expert", 1)},
        )

    def back_on(m, by):
        e = peer("expert", by)
        return remote(
            ret_send.at[m, e], ret_recv.at[0, m, me_e], back_send.at[m], back_recv.at[0, m],
            {"expert": e, "section": peer("section", 1)},
        )

    def back_on_all(m):
        return remote(
            ret_send.at[m], ret_recv.at[0, m], back_send.at[m], back_recv.at[0, m],
            {"section": peer("section", 1)},
        )

    def back_home(m, by):
        e = peer("expert", by)
        return remote(
            ret_send.at[m, e], ret_recv.at[1, m, me_e], back_send.at[m], back_recv.at[1, m],
            {"expert": e},
        )

    def back_far(m):
        return remote(
            ret_send.at[m, pl.ds(0, experts - 1)], ret_recv.at[1, m, pl.ds(0, experts - 1)],
            back_send.at[m], back_recv.at[1, m], {"expert": peer("expert", 1)},
        )

    def back_own(m):
        return pltpu.make_async_copy(
            ret_send.at[m, me_e], ret_recv.at[1, m, me_e], back_self.at[m]
        )

    def lanes(r):
        return pl.ds(pl.multiple_of(r * blk, blk), blk)

    def tail_line(e, j):
        return pl.ds(e * tail + j, blocks, stride=tails_all)

    def tail_part(j):
        return pl.ds(blocks + j * folds, folds)

    def put(dst, r, values):
        for e in range(experts):
            dst(e)[r] = values[e * main:(e + 1) * main].astype(BF16)
        tails_by[r] = values[experts * main:]

    def spread_tails(dst, e):
        for j in range(tail):
            lines = tails[tail_line(e, j), :].astype(BF16)
            dst(e)[tail_part(j)] = lines.reshape(folds, main, blk)

    def collect_tails(src):
        for e in range(experts):
            for j in range(tail):
                lines = src(e)[tail_part(j)].reshape(blocks, blk)
                tails[tail_line(e, j), :] = lines.astype(F32)

    def take(src, r):
        pieces_of = [src(e)[r] for e in range(experts)]
        return jnp.concatenate(pieces_of + [tails_by[r].astype(BF16)], axis=0)

    def dispatch(m):
        values = held[m].astype(F32)
        scale = lax.rsqrt(jnp.mean(values * values, axis=-1, keepdims=True) + EPS)
        normed[...] = (values * scale * gain[...]).astype(BF16)

        @pl.loop(0, blocks, unroll=8)
        def _(r):
            put(
                lambda e: send.at[m, e], r,
                jnp.dot(disp[m], normed[:, lanes(r)], preferred_element_type=F32),
            )

        for e in range(experts):
            spread_tails(lambda e: send.at[m, e], e)

    def send_chunks(m):
        for by in far_first:
            chunk_out(m, by).start()
        chunk_self(m).start()

    def segment(m, s, k):
        products = []
        start, size = cuts[k]
        for group in range(groups):
            for u in range(size):
                c = group * half + start + u
                at = groups * start + group * size + u
                x = take(lambda e: recv[m].at[e], meta_s[s, 0, c])
                gate = jnp.dot(x, weights[0, s, c], preferred_element_type=F32)
                up = jnp.dot(x, weights[1, s, c], preferred_element_type=F32)
                hidden = (gate / (1.0 + jnp.exp(-gate)) * up).astype(BF16)
                product = jnp.dot(hidden, weights[2, s, c], preferred_element_type=F32)
                products.append((at, c, product))
        for at, c, product in products:
            parts[s, at] = product + parts[s, meta_s[s, 1, c]]

    def expert_part(m, opening):
        chunk_self(m).wait()
        chunks_far(m).wait()
        collect_tails(lambda e: recv[m].at[e])
        if opening:
            mine = weights.at[:, me_s]
            pltpu.make_async_copy(mine, mine, own_sem).wait()
            for by in range(1, shards):
                meta_over_shard(by).wait()
            meta_own.wait()
            load = pltpu.make_async_copy(meta_v, meta_s, meta_copy_sem)
            load.start()
            load.wait()
            for k in range(len(cuts)):
                segment(m, me_s, k)
            for k in range(len(cuts)):
                @pl.when(first)
                def _():
                    finish_stage(k)

                @pl.when(me_l > 0)
                def _():
                    finish_relay(k)

                @pl.loop(1, shards)
                def _(by):
                    segment(m, peer("shard", shards - by), k)
        else:
            @pl.loop(0, shards)
            def _(s):
                for k in range(len(cuts)):
                    segment(m, s, k)

        @pl.loop(0, blocks, unroll=4)
        def _(j):
            total = parts[0, meta_s[0, 2, j]]
            for s in range(1, shards):
                total = total + parts[s, meta_s[s, 2, j]]
            put(lambda e: ret_send.at[m, e], j, total)

        for e in range(experts):
            spread_tails(lambda e: ret_send.at[m, e], e)

        @pl.when(me_l < sections - 1)
        def _():
            for by in far_first + [0]:
                back_on(m, by).start()

        @pl.when(last)
        def _():
            for by in far_first:
                back_home(m, by).start()
            back_own(m).start()

    def combine(m, which, dst):
        collect_tails(lambda e: ret_recv.at[which, m, e])

        @pl.loop(0, blocks, unroll=8)
        def _(r):
            mixed = jnp.dot(
                pieces[which, m], take(lambda e: ret_recv.at[which, m, e], r),
                preferred_element_type=F32,
            )
            mixed = mixed[:rows] + mixed[rows:2 * rows] + mixed[2 * rows:]
            dst[m, :, lanes(r)] = (held[m, :, lanes(r)].astype(F32) + mixed).astype(BF16)

    def split(which, m, value):
        for i in range(3):
            piece = value.astype(BF16)
            pieces[which, m, i * rows:(i + 1) * rows, :] = piece
            value = value - piece.astype(F32)

    def arrival(c):
        group = sum((c >= g * half).astype(jnp.int32) for g in range(1, groups))
        within = c - group * half
        start = sum(
            (within >= cuts[k][0]).astype(jnp.int32) * cuts[k - 1][1] for k in range(1, len(cuts))
        )
        size = cuts[0][1] + sum(
            (within >= cuts[k][0]).astype(jnp.int32) * (cuts[k][1] - cuts[k - 1][1])
            for k in range(1, len(cuts))
        )
        return (groups - 1) * start + group * size + within

    def iota(shape, axis):
        return lax.broadcasted_iota(jnp.int32, shape, axis)

    slot = iota((slots, rows), 0)
    inner = slot - experts * main
    head = inner < 0
    expert_main = sum((slot >= e * main).astype(jnp.int32) for e in range(1, experts))
    expert_tail = sum((inner >= e * tail).astype(jnp.int32) for e in range(1, experts + 1))
    expert = jnp.where(head, expert_main, expert_tail)
    place_in = jnp.where(head, slot - expert_main * main, main + inner - expert_tail * tail)
    place_in = place_in.astype(F32)
    earlier = (iota((rows, rows), 0) < iota((rows, rows), 1)).astype(F32).astype(BF16)
    for m in range(micro):
        named = [ids[m, j:j + 1, :] == expert for j in range(TOP)]
        hit = functools.reduce(jnp.logical_or, named)
        ahead = jnp.dot(
            hit.astype(F32).astype(BF16), earlier, preferred_element_type=F32
        )
        fits = hit & (ahead == place_in)
        amount = sum(jnp.where(named[j], mix[m, j:j + 1, :], 0.0) for j in range(TOP))
        disp[m] = fits.astype(F32).astype(BF16)
        comb[m] = jnp.transpose(jnp.where(fits, amount, 0.0))

    cols = cols_in[...]
    cols_down = jnp.transpose(jnp.broadcast_to(cols, (n_blk, n_blk)))
    from_place = arrival(iota((n_blk, n_blk), 0))
    chained = (cols_down == cols) & (from_place < arrival(iota((n_blk, n_blk), 1)))
    before = jnp.max(jnp.where(chained, from_place, -1), axis=0, keepdims=True)
    final = jnp.broadcast_to(cols_down[:, :1], (n_blk, blocks)) == iota((n_blk, blocks), 1)
    last_at = jnp.where(final, arrival(iota((n_blk, blocks), 0)), -1)
    last_at = jnp.max(last_at, axis=0, keepdims=True)
    meta_here[...] = jnp.zeros_like(meta_here)
    meta_here[0:1, 0:n_blk] = rows_in[...]
    meta_here[1:2, 0:n_blk] = jnp.where(before < 0, n_blk, before)
    meta_here[2:3, 0:blocks] = jnp.where(last_at < 0, n_blk, last_at)
    for s in range(shards):
        parts[s, n_blk] = jnp.zeros_like(parts[s, n_blk])

    for m in range(micro):
        token_copy(m).wait()

    @pl.when(first)
    def _():
        dispatch(0)

    @pl.when(last)
    def _():
        for m in range(micro):
            split(1, m, comb[m])

    pl.semaphore_wait(barrier, greeted)

    for by in range(1, shards):
        meta_over_shard(by).start()
    meta_own.start()

    @pl.when(first)
    def _():
        start_stage()
        send_chunks(0)

    @pl.when(me_l < sections - 1)
    def _():
        comb_copy().start()

    @pl.when(first)
    def _():
        for m in range(1, micro):
            dispatch(m)
            send_chunks(m)

    @pl.when(me_l > 0)
    def _():
        for k, by in pairs:
            stage_in(k, by).wait_recv()
            for hop in range(1, groups):
                stage_over(k, by, hop, me_g).start()
            stage_down(k, by).start()
        start_weights()
        comb_copy().wait_recv()
        for m in range(micro):
            split(0, m, comb_in[m])
        for m in range(micro):
            if m == 0:
                relay_weights(0, len(cuts) if micro == 1 else len(cuts) - 1)
            if m == 1:
                relay_weights(len(cuts) - 1, len(cuts))
            back_on_all(m).wait_recv()
            combine(m, 0, held)
            hand_back(m).start()
            dispatch(m)
            send_chunks(m)

    for m in range(micro):
        expert_part(m, m == 0)

    @pl.when(last)
    def _():
        for m in range(micro):
            back_own(m).wait()
            back_far(m).wait()
            combine(m, 1, out)

    @pl.when(me_l > 0)
    def _():
        for m in range(micro):
            hand_back(m).wait_send()
        all_sent(wx_send)
        all_sent(sc_send)
        for hop in range(1, groups):
            all_sent(sy_send.at[hop - 1])
            all_sent(wy_send.at[hop - 1])

    @pl.when(me_l < sections - 1)
    def _():
        comb_copy().wait_send()
        all_sent(sx_send)
        for m in range(micro):
            back_on_all(m).wait_send()
            hand_back(m).wait_recv()


def body(
    sizes,
    tokens,
    norm_gain,
    route_ids,
    route_weights,
    gate_blocks,
    up_blocks,
    down_blocks,
    gate_rows,
    down_cols,
):
    groups, shards, experts, sections = sizes
    assert sections == 2
    micro, rows, width = tokens.shape
    n_blk, blk = gate_blocks.shape[2], gate_blocks.shape[-1]
    blocks = width // blk
    cap = min(rows, max(rows * 9 // 16, rows * TOP // experts + 2))
    main = cap // 16 * 16
    tails_all = -(-(experts * (cap - main)) // 8) * 8
    slots = experts * main + tails_all

    cuts = len(cut_list(n_blk // groups))
    meta_width = -(-max(n_blk, blocks) // 128) * 128
    dims = (micro, rows, blocks, blk, cap, experts, shards, groups, sections, n_blk)
    dma = pltpu.SemaphoreType.DMA
    assert blocks % main == 0
    chunk = (micro, experts, cap * blocks // main, main, blk)
    vmem, anywhere = pl.BlockSpec(memory_space=pltpu.VMEM), pl.BlockSpec(memory_space=pltpu.HBM)
    out = pl.pallas_call(
        functools.partial(layer_kernel, dims),
        out_shape=pltpu.VMEM((micro, rows, width), BF16),
        in_specs=[anywhere] + [vmem] * 3 + [anywhere] * 3 + [vmem] * 2,
        out_specs=vmem,
        scratch_shapes=[
            pltpu.VMEM((micro, rows, width), BF16),
            pltpu.VMEM((micro, slots, rows), BF16),
            pltpu.VMEM((micro, rows, slots), F32),
            pltpu.VMEM((micro, rows, slots), F32),
            pltpu.VMEM((2, micro, 3 * rows, slots), BF16),
            pltpu.VMEM((8, meta_width), jnp.int32),
            pltpu.VMEM((rows, width), BF16),
            pltpu.VMEM((tails_all * blocks, blk), F32),
            pltpu.VMEM(chunk, BF16),
            [pltpu.VMEM(chunk[1:], BF16) for _ in range(micro)],
            pltpu.VMEM((shards, n_blk + 1, slots, blk), F32),
            pltpu.VMEM(chunk, BF16),
            pltpu.VMEM((2,) + chunk, BF16),
            pltpu.VMEM((3, shards, n_blk, blk, blk), BF16),
            pltpu.VMEM((3, shards, n_blk // groups, blk, blk), BF16),
            pltpu.VMEM((shards, 8, meta_width), jnp.int32),
            pltpu.SMEM((shards, 8, meta_width), jnp.int32),
            dma((micro,)),
            dma((2, micro)),
            dma,
            dma,
            dma((shards - 1,)),
            dma((shards - 1,)),
            dma,
            dma((2,)),
            dma,
            dma((cuts, shards - 1)),
            dma((groups - 1,)),
            dma((cuts, shards - 1, groups - 1)),
            dma((micro,)),
            dma((micro,)),
            dma((micro,)),
            dma((micro,)),
            dma((2, micro)),
            dma((micro,)),
            dma,
            dma((cuts, shards - 1)),
            dma,
            dma((cuts, shards - 1)),
            dma((groups - 1,)),
            dma((cuts, shards - 1, groups - 1)),
        ],
        compiler_params=pltpu.CompilerParams(
            collective_id=0, has_side_effects=True, vmem_limit_bytes=56 * 1024 * 1024
        ),
    )(
        tokens, norm_gain, jnp.swapaxes(route_ids[0], 1, 2), jnp.swapaxes(route_weights[0], 1, 2),
        gate_blocks.reshape(n_blk, blk, blk), up_blocks.reshape(n_blk, blk, blk),
        down_blocks.reshape(n_blk, blk, blk), gate_rows.reshape(1, n_blk),
        down_cols.reshape(1, n_blk),
    )
    return out[None]


def solution(mesh):
    sizes = tuple(mesh.shape[name] for name in ("groups", "shard", "expert", "section"))
    in_specs = (
        P(None, ("groups", "shard", "expert"), None),
        P("section", None),
        P("section", None, ("groups", "shard", "expert"), None),
        P("section", None, ("groups", "shard", "expert"), None),
        P("section", "expert", "shard", None, None, None),
        P("section", "expert", "shard", None, None, None),
        P("section", "expert", "shard", None, None, None),
        P("section", "expert", "shard", None),
        P("section", "expert", "shard", None),
    )
    out_specs = P("section", None, ("groups", "shard", "expert"), None)
    return jax.shard_map(
        functools.partial(body, sizes), mesh=mesh, in_specs=in_specs, out_specs=out_specs,
        check_vma=False,
    )
```

```python
import functools
import math

import jax
import jax.numpy as jnp
from jax import lax
from jax.experimental import pallas as pl
from jax.experimental.pallas import tpu as pltpu
from jax.sharding import PartitionSpec as P

TOP = 2
EPS = 1e-05
BF16 = jnp.bfloat16
F32 = jnp.float32
MOST = 2
RUN = 4


def cut_list(half):
    cuts, at = [], 0
    while at < half:
        size = min(MOST, at + 1, (half - at + 1) // 2)
        cuts.append((at, size))
        at += size
    return cuts


def layer_kernel(
    dims,
    tokens, gain, ids, mix, gate_hbm, up_hbm, down_hbm, rows_in, cols_in,
    out,
    held, disp, comb, comb_in, pieces, meta_here, normed, tails, send, recv, parts, ret_send, ret_recv,
    weights, stage, meta_v, meta_s,
    tok_sem, hand_sem, own_sem, meta_own_sem, meta_send_sem, meta_recv_sem, meta_copy_sem, comb_sem,
    wx_send, wx_recv, wy_send, wy_recv, disp_send, disp_recv, disp_self,
    back_send, back_recv, back_self, sx_send, sx_recv, sc_send, sc_recv, sy_send, sy_recv,
):
    micro, rows, blocks, blk, cap, experts, shards, groups, sections, n_blk = dims
    main = cap // 16 * 16
    tail = cap - main
    tails_all = -(-(experts * tail) // 8) * 8
    slots = experts * main + tails_all
    folds = blocks // main
    tails_by = tails.reshape(blocks, tails_all, blk)
    me_g, me_s = lax.axis_index("groups"), lax.axis_index("shard")
    me_e, me_l = lax.axis_index("expert"), lax.axis_index("section")
    sizes = {"groups": groups, "shard": shards, "expert": experts, "section": sections}
    place = {"groups": me_g, "shard": me_s, "expert": me_e, "section": me_l}
    half = n_blk // groups
    cuts = cut_list(half)
    sources = (gate_hbm, up_hbm, down_hbm)
    first, last = me_l == 0, me_l == sections - 1

    def remote(src, dst, ssem, rsem, device):
        return pltpu.make_async_remote_copy(
            src_ref=src, dst_ref=dst, send_sem=ssem, recv_sem=rsem,
            device_id=device, device_id_type=pl.DeviceIdType.MESH,
        )

    def peer(axis, by):
        return lax.rem(place[axis] + by, sizes[axis])

    def signal(sem, device):
        pl.semaphore_signal(sem, inc=1, device_id=device, device_id_type=pl.DeviceIdType.MESH)

    barrier = pltpu.get_barrier_semaphore()
    for axis in ("expert", "shard", "groups"):
        for by in range(sizes[axis] - 1, 0, -1):
            for hop in range(sections):
                signal(barrier, {axis: peer(axis, by), "section": peer("section", hop)})
    for hop in range(1, sections):
        signal(barrier, {"section": peer("section", hop)})
    greeted = sections * (groups + shards + experts - 2) - 1

    def token_copy(m):
        return pltpu.make_async_copy(tokens.at[m], held.at[m], tok_sem.at[m])

    for m in range(micro):
        token_copy(m).start()
    for a in range(3):
        pltpu.make_async_copy(sources[a], weights.at[a, me_s], own_sem).start()

    meta_own = pltpu.make_async_copy(meta_here, meta_v.at[me_s], meta_own_sem)

    def hand_back(m):
        return remote(
            held.at[m], out.at[m], hand_sem.at[0, m], hand_sem.at[1, m],
            {"section": peer("section", sections - 1)},
        )

    def comb_copy():
        return remote(
            comb, comb_in, comb_sem.at[0], comb_sem.at[1], {"section": peer("section", 1)}
        )

    def spot(group, k, shard):
        return weights.at[:, shard, pl.ds(group * half + cuts[k][0], cuts[k][1])]

    def staged(k, shard):
        return stage.at[:, shard, pl.ds(*cuts[k])]

    def origin(by):
        return peer("shard", shards - by)

    def own_part(a, k):
        return sources[a].at[pl.ds(me_g * half + cuts[k][0], cuts[k][1])]

    pairs = [(k, by) for k in range(len(cuts)) for by in range(1, shards)]
    others = stage.at[:, pl.ds(0, shards - 1)]

    def start_stage():
        for k, by in pairs:
            for a in range(3):
                remote(
                    own_part(a, k), stage.at[a, me_s, pl.ds(*cuts[k])], sx_send,
                    sx_recv.at[k, by - 1],
                    {"shard": peer("shard", by), "section": peer("section", 1)},
                ).start()

    def stage_in(k, by):
        at = staged(k, origin(by))
        return remote(at, at, sx_send, sx_recv.at[k, by - 1], {"section": peer("section", 1)})

    def stage_down(k, by):
        return remote(
            staged(k, origin(by)), spot(me_g, k, origin(by)), sc_send, sc_recv.at[k, by - 1],
            {"section": peer("section", 1)},
        )

    def stage_over(k, by, hop, from_g):
        return remote(
            staged(k, origin(by)), spot(from_g, k, origin(by)), sy_send.at[hop - 1],
            sy_recv.at[k, by - 1, hop - 1],
            {"groups": peer("groups", hop), "section": peer("section", 1)},
        )

    def start_weights():
        for k, by in pairs:
            for a in range(3):
                remote(
                    own_part(a, k),
                    weights.at[a, me_s, pl.ds(me_g * half + cuts[k][0], cuts[k][1])],
                    wx_send, wx_recv.at[k, by - 1], {"shard": peer("shard", by)},
                ).start()

    def weights_in(k, by):
        at = spot(me_g, k, origin(by))
        return remote(at, at, wx_send, wx_recv.at[k, by - 1], {"shard": peer("shard", by)})

    def weights_over(k, by, hop, from_g):
        at = spot(from_g, k, origin(by))
        return remote(
            at, at, wy_send.at[hop - 1], wy_recv.at[k, by - 1, hop - 1],
            {"groups": peer("groups", hop)},
        )

    def all_sent(sem):
        remote(others, others, sem, wx_recv.at[0, 0], {"shard": peer("shard", 1)}).wait_send()

    def meta_over_shard(by):
        return remote(
            meta_here, meta_v.at[me_s], meta_send_sem.at[by - 1], meta_recv_sem.at[by - 1],
            {"shard": peer("shard", by)},
        )

    def relay_weights(begin, end):
        for k, by in pairs:
            if begin <= k < end:
                weights_in(k, by).wait_recv()
                for hop in range(1, groups):
                    weights_over(k, by, hop, me_g).start()

    def finish_relay(at):
        for k, by in pairs:
            if k == at:
                for hop in range(1, groups):
                    weights_over(k, by, hop, peer("groups", groups - hop)).wait_recv()

    def finish_stage(at):
        for k, by in pairs:
            if k == at:
                stage_down(k, by).wait_recv()
                for hop in range(1, groups):
                    stage_over(k, by, hop, peer("groups", groups - hop)).wait_recv()

    far_first = sorted(range(1, experts), key=lambda by: abs(by - experts // 2))

    def chunk_out(m, by):
        e = peer("expert", by)
        return remote(
            send.at[m, e], recv[m].at[me_e], disp_send.at[m], disp_recv.at[m], {"expert": e}
        )

    def chunk_self(m):
        return pltpu.make_async_copy(send.at[m, me_e], recv[m].at[me_e], disp_self.at[m])

    def chunks_far(m):
        return remote(
            send.at[m, pl.ds(0, experts - 1)], recv[m].at[pl.ds(0, experts - 1)],
            disp_send.at[m], disp_recv.at[m], {"expert": peer("expert", 1)},
        )

    def back_on(m, by):
        e = peer("expert", by)
        return remote(
            ret_send.at[m, e], ret_recv.at[0, m, me_e], back_send.at[m], back_recv.at[0, m],
            {"expert": e, "section": peer("section", 1)},
        )

    def back_on_all(m):
        return remote(
            ret_send.at[m], ret_recv.at[0, m], back_send.at[m], back_recv.at[0, m],
            {"section": peer("section", 1)},
        )

    def back_home(m, by):
        e = peer("expert", by)
        return remote(
            ret_send.at[m, e], ret_recv.at[1, m, me_e], back_send.at[m], back_recv.at[1, m],
            {"expert": e},
        )

    def back_far(m):
        return remote(
            ret_send.at[m, pl.ds(0, experts - 1)], ret_recv.at[1, m, pl.ds(0, experts - 1)],
            back_send.at[m], back_recv.at[1, m], {"expert": peer("expert", 1)},
        )

    def back_own(m):
        return pltpu.make_async_copy(
            ret_send.at[m, me_e], ret_recv.at[1, m, me_e], back_self.at[m]
        )

    def lanes(r):
        return pl.ds(pl.multiple_of(r * blk, blk), blk)

    def tail_line(e, j):
        return pl.ds(e * tail + j, blocks, stride=tails_all)

    def tail_part(j):
        return pl.ds(blocks + j * folds, folds)

    def put(dst, r, values):
        for e in range(experts):
            dst(e)[r] = values[e * main:(e + 1) * main].astype(BF16)
        tails_by[r] = values[experts * main:]

    def spread_tails(dst, e):
        for j in range(tail):
            lines = tails[tail_line(e, j), :].astype(BF16)
            dst(e)[tail_part(j)] = lines.reshape(folds, main, blk)

    def collect_tails(src):
        for e in range(experts):
            for j in range(tail):
                lines = src(e)[tail_part(j)].reshape(blocks, blk)
                tails[tail_line(e, j), :] = lines.astype(F32)

    def take(src, r):
        pieces_of = [src(e)[r] for e in range(experts)]
        return jnp.concatenate(pieces_of + [tails_by[r].astype(BF16)], axis=0)

    def dispatch(m):
        values = held[m].astype(F32)
        scale = lax.rsqrt(jnp.mean(values * values, axis=-1, keepdims=True) + EPS)
        normed[...] = (values * scale * gain[...]).astype(BF16)

        @pl.loop(0, blocks, unroll=8)
        def _(r):
            put(
                lambda e: send.at[m, e], r,
                jnp.dot(disp[m], normed[:, lanes(r)], preferred_element_type=F32),
            )

        for e in range(experts):
            spread_tails(lambda e: send.at[m, e], e)

    def send_chunks(m):
        for by in far_first:
            chunk_out(m, by).start()
        chunk_self(m).start()

    def listed(k):
        start, size = cuts[k]
        return [
            (group * half + start + u, groups * start + group * size + u)
            for group in range(groups) for u in range(size)
        ]

    whole = [item for k in range(len(cuts)) for item in listed(k)]

    def segments(m, s, items):
        for i in range(0, len(items), RUN):
            segment(m, s, items[i:i + RUN])

    def segment(m, s, items):
        products = []
        for c, at in items:
            x = take(lambda e: recv[m].at[e], meta_s[s, 0, c])
            gate = jnp.dot(x, weights[0, s, c], preferred_element_type=F32)
            up = jnp.dot(x, weights[1, s, c], preferred_element_type=F32)
            hidden = (gate / (1.0 + jnp.exp(-gate)) * up).astype(BF16)
            product = jnp.dot(hidden, weights[2, s, c], preferred_element_type=F32)
            products.append((at, c, product))
        for at, c, product in products:
            parts[s, at] = product + parts[s, meta_s[s, 1, c]]

    def expert_part(m, opening):
        chunk_self(m).wait()
        chunks_far(m).wait()
        collect_tails(lambda e: recv[m].at[e])
        if opening:
            mine = weights.at[:, me_s]
            pltpu.make_async_copy(mine, mine, own_sem).wait()
            for by in range(1, shards):
                meta_over_shard(by).wait()
            meta_own.wait()
            load = pltpu.make_async_copy(meta_v, meta_s, meta_copy_sem)
            load.start()
            load.wait()
            segments(m, me_s, whole)
            for k in range(len(cuts)):
                @pl.when(first)
                def _():
                    finish_stage(k)

                @pl.when(me_l > 0)
                def _():
                    finish_relay(k)

                @pl.loop(1, shards)
                def _(by):
                    segments(m, peer("shard", shards - by), listed(k))
        else:
            @pl.loop(0, shards)
            def _(s):
                segments(m, s, whole)

        @pl.loop(0, blocks, unroll=4)
        def _(j):
            total = parts[0, meta_s[0, 2, j]]
            for s in range(1, shards):
                total = total + parts[s, meta_s[s, 2, j]]
            put(lambda e: ret_send.at[m, e], j, total)

        for e in range(experts):
            spread_tails(lambda e: ret_send.at[m, e], e)

        @pl.when(me_l < sections - 1)
        def _():
            for by in far_first + [0]:
                back_on(m, by).start()

        @pl.when(last)
        def _():
            for by in far_first:
                back_home(m, by).start()
            back_own(m).start()

    def combine(m, which, dst):
        collect_tails(lambda e: ret_recv.at[which, m, e])

        @pl.loop(0, blocks, unroll=8)
        def _(r):
            mixed = jnp.dot(
                pieces[which, m], take(lambda e: ret_recv.at[which, m, e], r),
                preferred_element_type=F32,
            )
            mixed = mixed[:rows] + mixed[rows:2 * rows] + mixed[2 * rows:]
            dst[m, :, lanes(r)] = (held[m, :, lanes(r)].astype(F32) + mixed).astype(BF16)

    def split(which, m, value):
        for i in range(3):
            piece = value.astype(BF16)
            pieces[which, m, i * rows:(i + 1) * rows, :] = piece
            value = value - piece.astype(F32)

    def arrival(c):
        group = sum((c >= g * half).astype(jnp.int32) for g in range(1, groups))
        within = c - group * half
        start = sum(
            (within >= cuts[k][0]).astype(jnp.int32) * cuts[k - 1][1] for k in range(1, len(cuts))
        )
        size = cuts[0][1] + sum(
            (within >= cuts[k][0]).astype(jnp.int32) * (cuts[k][1] - cuts[k - 1][1])
            for k in range(1, len(cuts))
        )
        return (groups - 1) * start + group * size + within

    def iota(shape, axis):
        return lax.broadcasted_iota(jnp.int32, shape, axis)

    slot = iota((slots, rows), 0)
    inner = slot - experts * main
    head = inner < 0
    expert_main = sum((slot >= e * main).astype(jnp.int32) for e in range(1, experts))
    expert_tail = sum((inner >= e * tail).astype(jnp.int32) for e in range(1, experts + 1))
    expert = jnp.where(head, expert_main, expert_tail)
    place_in = jnp.where(head, slot - expert_main * main, main + inner - expert_tail * tail)
    place_in = place_in.astype(F32)
    earlier = (iota((rows, rows), 0) < iota((rows, rows), 1)).astype(F32).astype(BF16)
    for m in range(micro):
        named = [ids[m, j:j + 1, :] == expert for j in range(TOP)]
        hit = functools.reduce(jnp.logical_or, named)
        ahead = jnp.dot(
            hit.astype(F32).astype(BF16), earlier, preferred_element_type=F32
        )
        fits = hit & (ahead == place_in)
        amount = sum(jnp.where(named[j], mix[m, j:j + 1, :], 0.0) for j in range(TOP))
        disp[m] = fits.astype(F32).astype(BF16)
        comb[m] = jnp.transpose(jnp.where(fits, amount, 0.0))

    cols = cols_in[...]
    cols_down = jnp.transpose(jnp.broadcast_to(cols, (n_blk, n_blk)))
    from_place = arrival(iota((n_blk, n_blk), 0))
    chained = (cols_down == cols) & (from_place < arrival(iota((n_blk, n_blk), 1)))
    before = jnp.max(jnp.where(chained, from_place, -1), axis=0, keepdims=True)
    final = jnp.broadcast_to(cols_down[:, :1], (n_blk, blocks)) == iota((n_blk, blocks), 1)
    last_at = jnp.where(final, arrival(iota((n_blk, blocks), 0)), -1)
    last_at = jnp.max(last_at, axis=0, keepdims=True)
    meta_here[...] = jnp.zeros_like(meta_here)
    meta_here[0:1, 0:n_blk] = rows_in[...]
    meta_here[1:2, 0:n_blk] = jnp.where(before < 0, n_blk, before)
    meta_here[2:3, 0:blocks] = jnp.where(last_at < 0, n_blk, last_at)
    for s in range(shards):
        parts[s, n_blk] = jnp.zeros_like(parts[s, n_blk])

    for m in range(micro):
        token_copy(m).wait()

    @pl.when(first)
    def _():
        dispatch(0)

    @pl.when(last)
    def _():
        for m in range(micro):
            split(1, m, comb[m])

    pl.semaphore_wait(barrier, greeted)

    for by in range(1, shards):
        meta_over_shard(by).start()
    meta_own.start()

    @pl.when(first)
    def _():
        start_stage()
        send_chunks(0)

    @pl.when(me_l < sections - 1)
    def _():
        comb_copy().start()

    @pl.when(first)
    def _():
        for m in range(1, micro):
            dispatch(m)
            send_chunks(m)

    @pl.when(me_l > 0)
    def _():
        for k, by in pairs:
            stage_in(k, by).wait_recv()
            for hop in range(1, groups):
                stage_over(k, by, hop, me_g).start()
            stage_down(k, by).start()
        start_weights()
        comb_copy().wait_recv()
        for m in range(micro):
            split(0, m, comb_in[m])
        for m in range(micro):
            if m == 0:
                relay_weights(0, len(cuts) if micro == 1 else len(cuts) - 1)
            if m == 1:
                relay_weights(len(cuts) - 1, len(cuts))
            back_on_all(m).wait_recv()
            combine(m, 0, held)
            hand_back(m).start()
            dispatch(m)
            send_chunks(m)

    for m in range(micro):
        expert_part(m, m == 0)

    @pl.when(last)
    def _():
        for m in range(micro):
            back_own(m).wait()
            back_far(m).wait()
            combine(m, 1, out)

    @pl.when(me_l > 0)
    def _():
        for m in range(micro):
            hand_back(m).wait_send()
        all_sent(wx_send)
        all_sent(sc_send)
        for hop in range(1, groups):
            all_sent(sy_send.at[hop - 1])
            all_sent(wy_send.at[hop - 1])

    @pl.when(me_l < sections - 1)
    def _():
        comb_copy().wait_send()
        all_sent(sx_send)
        for m in range(micro):
            back_on_all(m).wait_send()
            hand_back(m).wait_recv()


def body(
    sizes,
    tokens,
    norm_gain,
    route_ids,
    route_weights,
    gate_blocks,
    up_blocks,
    down_blocks,
    gate_rows,
    down_cols,
):
    groups, shards, experts, sections = sizes
    assert sections == 2
    micro, rows, width = tokens.shape
    n_blk, blk = gate_blocks.shape[2], gate_blocks.shape[-1]
    blocks = width // blk
    cap = min(rows, max(rows * 9 // 16, rows * TOP // experts + 2))
    main = cap // 16 * 16
    tails_all = -(-(experts * (cap - main)) // 8) * 8
    slots = experts * main + tails_all

    cuts = len(cut_list(n_blk // groups))
    meta_width = -(-max(n_blk, blocks) // 128) * 128
    dims = (micro, rows, blocks, blk, cap, experts, shards, groups, sections, n_blk)
    dma = pltpu.SemaphoreType.DMA
    assert blocks % main == 0
    chunk = (micro, experts, cap * blocks // main, main, blk)
    vmem, anywhere = pl.BlockSpec(memory_space=pltpu.VMEM), pl.BlockSpec(memory_space=pltpu.HBM)
    out = pl.pallas_call(
        functools.partial(layer_kernel, dims),
        out_shape=pltpu.VMEM((micro, rows, width), BF16),
        in_specs=[anywhere] + [vmem] * 3 + [anywhere] * 3 + [vmem] * 2,
        out_specs=vmem,
        scratch_shapes=[
            pltpu.VMEM((micro, rows, width), BF16),
            pltpu.VMEM((micro, slots, rows), BF16),
            pltpu.VMEM((micro, rows, slots), F32),
            pltpu.VMEM((micro, rows, slots), F32),
            pltpu.VMEM((2, micro, 3 * rows, slots), BF16),
            pltpu.VMEM((8, meta_width), jnp.int32),
            pltpu.VMEM((rows, width), BF16),
            pltpu.VMEM((tails_all * blocks, blk), F32),
            pltpu.VMEM(chunk, BF16),
            [pltpu.VMEM(chunk[1:], BF16) for _ in range(micro)],
            pltpu.VMEM((shards, n_blk + 1, slots, blk), F32),
            pltpu.VMEM(chunk, BF16),
            pltpu.VMEM((2,) + chunk, BF16),
            pltpu.VMEM((3, shards, n_blk, blk, blk), BF16),
            pltpu.VMEM((3, shards, n_blk // groups, blk, blk), BF16),
            pltpu.VMEM((shards, 8, meta_width), jnp.int32),
            pltpu.SMEM((shards, 8, meta_width), jnp.int32),
            dma((micro,)),
            dma((2, micro)),
            dma,
            dma,
            dma((shards - 1,)),
            dma((shards - 1,)),
            dma,
            dma((2,)),
            dma,
            dma((cuts, shards - 1)),
            dma((groups - 1,)),
            dma((cuts, shards - 1, groups - 1)),
            dma((micro,)),
            dma((micro,)),
            dma((micro,)),
            dma((micro,)),
            dma((2, micro)),
            dma((micro,)),
            dma,
            dma((cuts, shards - 1)),
            dma,
            dma((cuts, shards - 1)),
            dma((groups - 1,)),
            dma((cuts, shards - 1, groups - 1)),
        ],
        compiler_params=pltpu.CompilerParams(
            collective_id=0, has_side_effects=True, vmem_limit_bytes=56 * 1024 * 1024
        ),
    )(
        tokens, norm_gain, jnp.swapaxes(route_ids[0], 1, 2), jnp.swapaxes(route_weights[0], 1, 2),
        gate_blocks.reshape(n_blk, blk, blk), up_blocks.reshape(n_blk, blk, blk),
        down_blocks.reshape(n_blk, blk, blk), gate_rows.reshape(1, n_blk),
        down_cols.reshape(1, n_blk),
    )
    return out[None]


def solution(mesh):
    sizes = tuple(mesh.shape[name] for name in ("groups", "shard", "expert", "section"))
    in_specs = (
        P(None, ("groups", "shard", "expert"), None),
        P("section", None),
        P("section", None, ("groups", "shard", "expert"), None),
        P("section", None, ("groups", "shard", "expert"), None),
        P("section", "expert", "shard", None, None, None),
        P("section", "expert", "shard", None, None, None),
        P("section", "expert", "shard", None, None, None),
        P("section", "expert", "shard", None),
        P("section", "expert", "shard", None),
    )
    out_specs = P("section", None, ("groups", "shard", "expert"), None)
    return jax.shard_map(
        functools.partial(body, sizes), mesh=mesh, in_specs=in_specs, out_specs=out_specs,
        check_vma=False,
    )
```

```python
import functools
import math

import jax
import jax.numpy as jnp
from jax import lax
from jax.experimental import pallas as pl
from jax.experimental.pallas import tpu as pltpu
from jax.sharding import PartitionSpec as P

TOP = 2
EPS = 1e-05
BF16 = jnp.bfloat16
F32 = jnp.float32
MOST = 2
RUN = 4


def both_ways(half, groups):
    return half // 16 if groups > 1 else 0


def cut_list(keep):
    cuts, at = [], 0
    while at < keep:
        size = min(MOST, at + 1, (keep - at + 1) // 2)
        cuts.append((at, size))
        at += size
    return cuts


def layer_kernel(
    dims,
    tokens, gain, ids, mix, gate_hbm, up_hbm, down_hbm, rows_in, cols_in,
    out,
    held, disp, comb, comb_in, pieces, meta_here, normed, tails, send, recv, parts, ret_send, ret_recv,
    weights, stage, meta_v, meta_s,
    tok_sem, hand_sem, own_sem, meta_own_sem, meta_send_sem, meta_recv_sem, meta_copy_sem, comb_sem,
    wx_send, wx_recv, wy_send, wy_recv, disp_send, disp_recv, disp_self,
    back_send, back_recv, back_self, sx_send, sx_recv, sc_send, sc_recv, sy_send, sy_recv,
):
    micro, rows, blocks, blk, cap, experts, shards, groups, sections, n_blk = dims
    main = cap // 16 * 16
    tail = cap - main
    tails_all = -(-(experts * tail) // 8) * 8
    slots = experts * main + tails_all
    folds = blocks // main
    tails_by = tails.reshape(blocks, tails_all, blk)
    me_g, me_s = lax.axis_index("groups"), lax.axis_index("shard")
    me_e, me_l = lax.axis_index("expert"), lax.axis_index("section")
    sizes = {"groups": groups, "shard": shards, "expert": experts, "section": sections}
    place = {"groups": me_g, "shard": me_s, "expert": me_e, "section": me_l}
    half = n_blk // groups
    extra = both_ways(half, groups)
    keep = half - extra
    cuts = cut_list(keep)
    sources = (gate_hbm, up_hbm, down_hbm)
    pieces_in = len(cuts) + min(extra, 1)
    first, last = me_l == 0, me_l == sections - 1

    def remote(src, dst, ssem, rsem, device):
        return pltpu.make_async_remote_copy(
            src_ref=src, dst_ref=dst, send_sem=ssem, recv_sem=rsem,
            device_id=device, device_id_type=pl.DeviceIdType.MESH,
        )

    def peer(axis, by):
        return lax.rem(place[axis] + by, sizes[axis])

    def signal(sem, device):
        pl.semaphore_signal(sem, inc=1, device_id=device, device_id_type=pl.DeviceIdType.MESH)

    barrier = pltpu.get_barrier_semaphore()
    for axis in ("expert", "shard", "groups"):
        for by in range(sizes[axis] - 1, 0, -1):
            for hop in range(sections):
                signal(barrier, {axis: peer(axis, by), "section": peer("section", hop)})
    for hop in range(1, sections):
        signal(barrier, {"section": peer("section", hop)})
    greeted = sections * (groups + shards + experts - 2) - 1

    def token_copy(m):
        return pltpu.make_async_copy(tokens.at[m], held.at[m], tok_sem.at[m])

    for m in range(micro):
        token_copy(m).start()
    for a in range(3):
        pltpu.make_async_copy(sources[a], weights.at[a, me_s], own_sem).start()

    meta_own = pltpu.make_async_copy(meta_here, meta_v.at[me_s], meta_own_sem)

    def hand_back(m):
        return remote(
            held.at[m], out.at[m], hand_sem.at[0, m], hand_sem.at[1, m],
            {"section": peer("section", sections - 1)},
        )

    def comb_copy():
        return remote(
            comb, comb_in, comb_sem.at[0], comb_sem.at[1], {"section": peer("section", 1)}
        )

    def spot(group, k, shard):
        return weights.at[:, shard, pl.ds(group * half + cuts[k][0], cuts[k][1])]

    def staged(k, shard):
        if k == len(cuts):
            return stage.at[:, shard, pl.ds(keep, groups * extra)]
        return stage.at[:, shard, pl.ds(*cuts[k])]

    def origin(by):
        return peer("shard", shards - by)

    def outgoing(k):
        if k == len(cuts):
            return [(q * half + keep, keep + q * extra, extra) for q in range(groups)]
        return [(me_g * half + cuts[k][0], cuts[k][0], cuts[k][1])]

    relayed = [(k, by) for k in range(len(cuts)) for by in range(1, shards)]
    pairs = [(k, by) for k in range(pieces_in) for by in range(1, shards)]

    def start_stage():
        for k, by in pairs:
            for c, to, size in outgoing(k):
                remote(
                    weights.at[:, me_s, pl.ds(c, size)], stage.at[:, me_s, pl.ds(to, size)],
                    sx_send, sx_recv.at[k, by - 1],
                    {"shard": peer("shard", by), "section": peer("section", 1)},
                ).start()

    def stage_in(k, by):
        at = staged(k, origin(by))
        return remote(at, at, sx_send, sx_recv.at[k, by - 1], {"section": peer("section", 1)})

    def start_down(k, by):
        for c, to, size in outgoing(k):
            remote(
                stage.at[:, origin(by), pl.ds(to, size)],
                weights.at[:, origin(by), pl.ds(c, size)], sc_send, sc_recv.at[k, by - 1],
                {"section": peer("section", 1)},
            ).start()

    def stage_down(k, by):
        at = staged(k, origin(by))
        return remote(at, at, sc_send, sc_recv.at[k, by - 1], {"section": peer("section", 1)})

    def stage_over(k, by, hop, from_g):
        return remote(
            staged(k, origin(by)), spot(from_g, k, origin(by)), sy_send.at[hop - 1],
            sy_recv.at[k, by - 1, hop - 1],
            {"groups": peer("groups", hop), "section": peer("section", 1)},
        )

    def start_weights():
        for k, by in pairs:
            for c, to, size in outgoing(k):
                at = weights.at[:, me_s, pl.ds(c, size)]
                remote(
                    at, at, wx_send, wx_recv.at[k, by - 1], {"shard": peer("shard", by)}
                ).start()

    def weights_in(k, by):
        at = staged(k, origin(by))
        return remote(at, at, wx_send, wx_recv.at[k, by - 1], {"shard": peer("shard", by)})

    def weights_over(k, by, hop, from_g):
        at = spot(from_g, k, origin(by))
        return remote(
            at, at, wy_send.at[hop - 1], wy_recv.at[k, by - 1, hop - 1],
            {"groups": peer("groups", hop)},
        )

    def all_sent(sem, size=None):
        at = stage.at[:, pl.ds(0, shards - 1), pl.ds(0, size or keep + groups * extra)]
        remote(at, at, sem, wx_recv.at[0, 0], {"shard": peer("shard", 1)}).wait_send()

    def meta_over_shard(by):
        return remote(
            meta_here, meta_v.at[me_s], meta_send_sem.at[by - 1], meta_recv_sem.at[by - 1],
            {"shard": peer("shard", by)},
        )

    def relay_weights(begin, end):
        for k, by in pairs:
            if begin <= k < end:
                weights_in(k, by).wait_recv()
                if k < len(cuts):
                    for hop in range(1, groups):
                        weights_over(k, by, hop, me_g).start()

    def finish_relay(at):
        for k, by in relayed:
            if k == at:
                for hop in range(1, groups):
                    weights_over(k, by, hop, peer("groups", groups - hop)).wait_recv()

    def finish_stage(at):
        for k, by in pairs:
            if k == at:
                stage_down(k, by).wait_recv()
                if k < len(cuts):
                    for hop in range(1, groups):
                        stage_over(k, by, hop, peer("groups", groups - hop)).wait_recv()

    far_first = sorted(range(1, experts), key=lambda by: abs(by - experts // 2))

    def chunk_out(m, by):
        e = peer("expert", by)
        return remote(
            send.at[m, e], recv[m].at[me_e], disp_send.at[m], disp_recv.at[m], {"expert": e}
        )

    def chunk_self(m):
        return pltpu.make_async_copy(send.at[m, me_e], recv[m].at[me_e], disp_self.at[m])

    def chunks_far(m):
        return remote(
            send.at[m, pl.ds(0, experts - 1)], recv[m].at[pl.ds(0, experts - 1)],
            disp_send.at[m], disp_recv.at[m], {"expert": peer("expert", 1)},
        )

    def back_on(m, by):
        e = peer("expert", by)
        return remote(
            ret_send.at[m, e], ret_recv.at[0, m, me_e], back_send.at[m], back_recv.at[0, m],
            {"expert": e, "section": peer("section", 1)},
        )

    def back_on_all(m):
        return remote(
            ret_send.at[m], ret_recv.at[0, m], back_send.at[m], back_recv.at[0, m],
            {"section": peer("section", 1)},
        )

    def back_home(m, by):
        e = peer("expert", by)
        return remote(
            ret_send.at[m, e], ret_recv.at[1, m, me_e], back_send.at[m], back_recv.at[1, m],
            {"expert": e},
        )

    def back_far(m):
        return remote(
            ret_send.at[m, pl.ds(0, experts - 1)], ret_recv.at[1, m, pl.ds(0, experts - 1)],
            back_send.at[m], back_recv.at[1, m], {"expert": peer("expert", 1)},
        )

    def back_own(m):
        return pltpu.make_async_copy(
            ret_send.at[m, me_e], ret_recv.at[1, m, me_e], back_self.at[m]
        )

    def lanes(r):
        return pl.ds(pl.multiple_of(r * blk, blk), blk)

    def tail_line(e, j):
        return pl.ds(e * tail + j, blocks, stride=tails_all)

    def tail_part(j):
        return pl.ds(blocks + j * folds, folds)

    def put(dst, r, values):
        for e in range(experts):
            dst(e)[r] = values[e * main:(e + 1) * main].astype(BF16)
        tails_by[r] = values[experts * main:]

    def spread_tails(dst, e):
        for j in range(tail):
            lines = tails[tail_line(e, j), :].astype(BF16)
            dst(e)[tail_part(j)] = lines.reshape(folds, main, blk)

    def collect_tails(src):
        for e in range(experts):
            for j in range(tail):
                lines = src(e)[tail_part(j)].reshape(blocks, blk)
                tails[tail_line(e, j), :] = lines.astype(F32)

    def take(src, r):
        pieces_of = [src(e)[r] for e in range(experts)]
        return jnp.concatenate(pieces_of + [tails_by[r].astype(BF16)], axis=0)

    def dispatch(m):
        values = held[m].astype(F32)
        scale = lax.rsqrt(jnp.mean(values * values, axis=-1, keepdims=True) + EPS)
        normed[...] = (values * scale * gain[...]).astype(BF16)

        @pl.loop(0, blocks, unroll=8)
        def _(r):
            put(
                lambda e: send.at[m, e], r,
                jnp.dot(disp[m], normed[:, lanes(r)], preferred_element_type=F32),
            )

        for e in range(experts):
            spread_tails(lambda e: send.at[m, e], e)

    def send_chunks(m):
        for by in far_first:
            chunk_out(m, by).start()
        chunk_self(m).start()

    def listed(k):
        if k == len(cuts):
            return [
                (group * half + keep + u, groups * keep + group * extra + u)
                for group in range(groups) for u in range(extra)
            ]
        start, size = cuts[k]
        return [
            (group * half + start + u, groups * start + group * size + u)
            for group in range(groups) for u in range(size)
        ]

    whole = [item for k in range(pieces_in) for item in listed(k)]

    def segments(m, s, items):
        for i in range(0, len(items), RUN):
            segment(m, s, items[i:i + RUN])

    def segment(m, s, items):
        products = []
        for c, at in items:
            x = take(lambda e: recv[m].at[e], meta_s[s, 0, c])
            gate = jnp.dot(x, weights[0, s, c], preferred_element_type=F32)
            up = jnp.dot(x, weights[1, s, c], preferred_element_type=F32)
            hidden = (gate / (1.0 + jnp.exp(-gate)) * up).astype(BF16)
            product = jnp.dot(hidden, weights[2, s, c], preferred_element_type=F32)
            products.append((at, c, product))
        for at, c, product in products:
            parts[s, at] = product + parts[s, meta_s[s, 1, c]]

    def expert_part(m, opening):
        chunk_self(m).wait()
        chunks_far(m).wait()
        collect_tails(lambda e: recv[m].at[e])
        if opening:
            for by in range(1, shards):
                meta_over_shard(by).wait()
            meta_own.wait()
            load = pltpu.make_async_copy(meta_v, meta_s, meta_copy_sem)
            load.start()
            load.wait()
            segments(m, me_s, whole)
            for k in range(pieces_in):
                @pl.when(first)
                def _():
                    finish_stage(k)

                @pl.when(me_l > 0)
                def _():
                    finish_relay(k)

                @pl.loop(1, shards)
                def _(by):
                    segments(m, peer("shard", shards - by), listed(k))
        else:
            @pl.loop(0, shards)
            def _(s):
                segments(m, s, whole)

        @pl.loop(0, blocks, unroll=4)
        def _(j):
            total = parts[0, meta_s[0, 2, j]]
            for s in range(1, shards):
                total = total + parts[s, meta_s[s, 2, j]]
            put(lambda e: ret_send.at[m, e], j, total)

        for e in range(experts):
            spread_tails(lambda e: ret_send.at[m, e], e)

        @pl.when(me_l < sections - 1)
        def _():
            for by in far_first + [0]:
                back_on(m, by).start()

        @pl.when(last)
        def _():
            for by in far_first:
                back_home(m, by).start()
            back_own(m).start()

    def combine(m, which, dst):
        collect_tails(lambda e: ret_recv.at[which, m, e])

        @pl.loop(0, blocks, unroll=8)
        def _(r):
            mixed = jnp.dot(
                pieces[which, m], take(lambda e: ret_recv.at[which, m, e], r),
                preferred_element_type=F32,
            )
            mixed = mixed[:rows] + mixed[rows:2 * rows] + mixed[2 * rows:]
            dst[m, :, lanes(r)] = (held[m, :, lanes(r)].astype(F32) + mixed).astype(BF16)

    def split(which, m, value):
        for i in range(3):
            piece = value.astype(BF16)
            pieces[which, m, i * rows:(i + 1) * rows, :] = piece
            value = value - piece.astype(F32)

    def arrival(c):
        group = sum((c >= g * half).astype(jnp.int32) for g in range(1, groups))
        within = c - group * half
        start = sum(
            (within >= cuts[k][0]).astype(jnp.int32) * cuts[k - 1][1] for k in range(1, len(cuts))
        )
        size = cuts[0][1] + sum(
            (within >= cuts[k][0]).astype(jnp.int32) * (cuts[k][1] - cuts[k - 1][1])
            for k in range(1, len(cuts))
        )
        early = (groups - 1) * start + group * size + within
        return jnp.where(within < keep, early, groups * keep + group * extra + within - keep)

    def iota(shape, axis):
        return lax.broadcasted_iota(jnp.int32, shape, axis)

    slot = iota((slots, rows), 0)
    inner = slot - experts * main
    head = inner < 0
    expert_main = sum((slot >= e * main).astype(jnp.int32) for e in range(1, experts))
    expert_tail = sum((inner >= e * tail).astype(jnp.int32) for e in range(1, experts + 1))
    expert = jnp.where(head, expert_main, expert_tail)
    place_in = jnp.where(head, slot - expert_main * main, main + inner - expert_tail * tail)
    place_in = place_in.astype(F32)
    earlier = (iota((rows, rows), 0) < iota((rows, rows), 1)).astype(F32).astype(BF16)
    for m in range(micro):
        named = [ids[m, j:j + 1, :] == expert for j in range(TOP)]
        hit = functools.reduce(jnp.logical_or, named)
        ahead = jnp.dot(
            hit.astype(F32).astype(BF16), earlier, preferred_element_type=F32
        )
        fits = hit & (ahead == place_in)
        amount = sum(jnp.where(named[j], mix[m, j:j + 1, :], 0.0) for j in range(TOP))
        disp[m] = fits.astype(F32).astype(BF16)
        comb[m] = jnp.transpose(jnp.where(fits, amount, 0.0))

    cols = cols_in[...]
    cols_down = jnp.transpose(jnp.broadcast_to(cols, (n_blk, n_blk)))
    from_place = arrival(iota((n_blk, n_blk), 0))
    chained = (cols_down == cols) & (from_place < arrival(iota((n_blk, n_blk), 1)))
    before = jnp.max(jnp.where(chained, from_place, -1), axis=0, keepdims=True)
    final = jnp.broadcast_to(cols_down[:, :1], (n_blk, blocks)) == iota((n_blk, blocks), 1)
    last_at = jnp.where(final, arrival(iota((n_blk, blocks), 0)), -1)
    last_at = jnp.max(last_at, axis=0, keepdims=True)
    meta_here[...] = jnp.zeros_like(meta_here)
    meta_here[0:1, 0:n_blk] = rows_in[...]
    meta_here[1:2, 0:n_blk] = jnp.where(before < 0, n_blk, before)
    meta_here[2:3, 0:blocks] = jnp.where(last_at < 0, n_blk, last_at)
    for s in range(shards):
        parts[s, n_blk] = jnp.zeros_like(parts[s, n_blk])

    for m in range(micro):
        token_copy(m).wait()

    @pl.when(first)
    def _():
        dispatch(0)

    @pl.when(last)
    def _():
        for m in range(micro):
            split(1, m, comb[m])

    mine = weights.at[:, me_s]
    pltpu.make_async_copy(mine, mine, own_sem).wait()
    pl.semaphore_wait(barrier, greeted)

    for by in range(1, shards):
        meta_over_shard(by).start()
    meta_own.start()

    @pl.when(first)
    def _():
        start_stage()
        send_chunks(0)

    @pl.when(me_l < sections - 1)
    def _():
        comb_copy().start()

    @pl.when(first)
    def _():
        for m in range(1, micro):
            dispatch(m)
            send_chunks(m)

    @pl.when(me_l > 0)
    def _():
        for k, by in pairs:
            stage_in(k, by).wait_recv()
            if k < len(cuts):
                for hop in range(1, groups):
                    stage_over(k, by, hop, me_g).start()
            start_down(k, by)
        start_weights()
        comb_copy().wait_recv()
        for m in range(micro):
            split(0, m, comb_in[m])
        for m in range(micro):
            if m == 0:
                relay_weights(0, pieces_in if micro == 1 else pieces_in - 2)
            if m == 1:
                relay_weights(max(0, pieces_in - 2), pieces_in)
            back_on_all(m).wait_recv()
            if m > 0:
                send_chunks(m - 1)
            combine(m, 0, held)
            hand_back(m).start()
            dispatch(m)
        send_chunks(micro - 1)

    for m in range(micro):
        expert_part(m, m == 0)

    @pl.when(last)
    def _():
        for m in range(micro):
            back_own(m).wait()
            back_far(m).wait()
            combine(m, 1, out)

    @pl.when(me_l > 0)
    def _():
        for m in range(micro):
            hand_back(m).wait_send()
        all_sent(wx_send)
        all_sent(sc_send)
        for hop in range(1, groups):
            all_sent(sy_send.at[hop - 1], keep)
            all_sent(wy_send.at[hop - 1], keep)

    @pl.when(me_l < sections - 1)
    def _():
        comb_copy().wait_send()
        all_sent(sx_send)
        for m in range(micro):
            back_on_all(m).wait_send()
            hand_back(m).wait_recv()


def body(
    sizes,
    tokens,
    norm_gain,
    route_ids,
    route_weights,
    gate_blocks,
    up_blocks,
    down_blocks,
    gate_rows,
    down_cols,
):
    groups, shards, experts, sections = sizes
    assert sections == 2
    micro, rows, width = tokens.shape
    n_blk, blk = gate_blocks.shape[2], gate_blocks.shape[-1]
    blocks = width // blk
    cap = min(rows, max(rows * 9 // 16, rows * TOP // experts + 2))
    main = cap // 16 * 16
    tails_all = -(-(experts * (cap - main)) // 8) * 8
    slots = experts * main + tails_all

    extra = both_ways(n_blk // groups, groups)
    keep = n_blk // groups - extra
    cuts = len(cut_list(keep)) + min(extra, 1)
    meta_width = -(-max(n_blk, blocks) // 128) * 128
    dims = (micro, rows, blocks, blk, cap, experts, shards, groups, sections, n_blk)
    dma = pltpu.SemaphoreType.DMA
    assert blocks % main == 0
    chunk = (micro, experts, cap * blocks // main, main, blk)
    vmem, anywhere = pl.BlockSpec(memory_space=pltpu.VMEM), pl.BlockSpec(memory_space=pltpu.HBM)
    out = pl.pallas_call(
        functools.partial(layer_kernel, dims),
        out_shape=pltpu.VMEM((micro, rows, width), BF16),
        in_specs=[anywhere] + [vmem] * 3 + [anywhere] * 3 + [vmem] * 2,
        out_specs=vmem,
        scratch_shapes=[
            pltpu.VMEM((micro, rows, width), BF16),
            pltpu.VMEM((micro, slots, rows), BF16),
            pltpu.VMEM((micro, rows, slots), F32),
            pltpu.VMEM((micro, rows, slots), F32),
            pltpu.VMEM((2, micro, 3 * rows, slots), BF16),
            pltpu.VMEM((8, meta_width), jnp.int32),
            pltpu.VMEM((rows, width), BF16),
            pltpu.VMEM((tails_all * blocks, blk), F32),
            pltpu.VMEM(chunk, BF16),
            [pltpu.VMEM(chunk[1:], BF16) for _ in range(micro)],
            pltpu.VMEM((shards, n_blk + 1, slots, blk), F32),
            pltpu.VMEM(chunk, BF16),
            pltpu.VMEM((2,) + chunk, BF16),
            pltpu.VMEM((3, shards, n_blk, blk, blk), BF16),
            pltpu.VMEM((3, shards, keep + groups * extra, blk, blk), BF16),
            pltpu.VMEM((shards, 8, meta_width), jnp.int32),
            pltpu.SMEM((shards, 8, meta_width), jnp.int32),
            dma((micro,)),
            dma((2, micro)),
            dma,
            dma,
            dma((shards - 1,)),
            dma((shards - 1,)),
            dma,
            dma((2,)),
            dma,
            dma((cuts, shards - 1)),
            dma((groups - 1,)),
            dma((cuts, shards - 1, groups - 1)),
            dma((micro,)),
            dma((micro,)),
            dma((micro,)),
            dma((micro,)),
            dma((2, micro)),
            dma((micro,)),
            dma,
            dma((cuts, shards - 1)),
            dma,
            dma((cuts, shards - 1)),
            dma((groups - 1,)),
            dma((cuts, shards - 1, groups - 1)),
        ],
        compiler_params=pltpu.CompilerParams(
            collective_id=0, has_side_effects=True, vmem_limit_bytes=56 * 1024 * 1024
        ),
    )(
        tokens, norm_gain, jnp.swapaxes(route_ids[0], 1, 2), jnp.swapaxes(route_weights[0], 1, 2),
        gate_blocks.reshape(n_blk, blk, blk), up_blocks.reshape(n_blk, blk, blk),
        down_blocks.reshape(n_blk, blk, blk), gate_rows.reshape(1, n_blk),
        down_cols.reshape(1, n_blk),
    )
    return out[None]


def solution(mesh):
    sizes = tuple(mesh.shape[name] for name in ("groups", "shard", "expert", "section"))
    in_specs = (
        P(None, ("groups", "shard", "expert"), None),
        P("section", None),
        P("section", None, ("groups", "shard", "expert"), None),
        P("section", None, ("groups", "shard", "expert"), None),
        P("section", "expert", "shard", None, None, None),
        P("section", "expert", "shard", None, None, None),
        P("section", "expert", "shard", None, None, None),
        P("section", "expert", "shard", None),
        P("section", "expert", "shard", None),
    )
    out_specs = P("section", None, ("groups", "shard", "expert"), None)
    return jax.shard_map(
        functools.partial(body, sizes), mesh=mesh, in_specs=in_specs, out_specs=out_specs,
        check_vma=False,
    )
```

```python
import functools
import math

import jax
import jax.numpy as jnp
from jax import lax
from jax.experimental import pallas as pl
from jax.experimental.pallas import tpu as pltpu
from jax.sharding import PartitionSpec as P

TOP = 2
EPS = 1e-05
BF16 = jnp.bfloat16
F32 = jnp.float32
MOST = 2
RUN = 4


def both_ways(half, groups):
    return half // 16 if groups > 1 else 0


def cut_list(keep):
    cuts, at = [], 0
    while at < keep:
        size = min(MOST, at + 1, (keep - at + 1) // 2)
        cuts.append((at, size))
        at += size
    return cuts


def layer_kernel(
    dims,
    tokens, gain, ids, mix, gate_hbm, up_hbm, down_hbm, rows_in, cols_in,
    out,
    held, disp, comb, comb_in, pieces, meta_here, normed, tails, send, recv, parts, ret_send, ret_recv,
    weights, stage, meta_v, meta_s,
    tok_sem, hand_sem, own_sem, meta_own_sem, meta_send_sem, meta_recv_sem, meta_copy_sem, comb_sem,
    wx_send, wx_recv, wy_send, wy_recv, disp_send, disp_recv, disp_self,
    back_send, back_recv, back_self, sx_send, sx_recv, sc_send, sc_recv, sy_send, sy_recv,
):
    micro, rows, blocks, blk, cap, experts, shards, groups, sections, n_blk = dims
    main = cap // 16 * 16
    tail = cap - main
    tails_all = -(-(experts * tail) // 8) * 8
    slots = experts * main + tails_all
    folds = blocks // main
    tails_by = tails.reshape(blocks, tails_all, blk)
    me_g, me_s = lax.axis_index("groups"), lax.axis_index("shard")
    me_e, me_l = lax.axis_index("expert"), lax.axis_index("section")
    sizes = {"groups": groups, "shard": shards, "expert": experts, "section": sections}
    place = {"groups": me_g, "shard": me_s, "expert": me_e, "section": me_l}
    half = n_blk // groups
    extra = both_ways(half, groups)
    keep = half - extra
    cuts = cut_list(keep)
    sources = (gate_hbm, up_hbm, down_hbm)
    pieces_in = len(cuts) + min(extra, 1)
    first, last = me_l == 0, me_l == sections - 1

    def remote(src, dst, ssem, rsem, device):
        return pltpu.make_async_remote_copy(
            src_ref=src, dst_ref=dst, send_sem=ssem, recv_sem=rsem,
            device_id=device, device_id_type=pl.DeviceIdType.MESH,
        )

    def peer(axis, by):
        return lax.rem(place[axis] + by, sizes[axis])

    def signal(sem, device):
        pl.semaphore_signal(sem, inc=1, device_id=device, device_id_type=pl.DeviceIdType.MESH)

    barrier = pltpu.get_barrier_semaphore()
    for axis in ("expert", "shard", "groups"):
        for by in range(sizes[axis] - 1, 0, -1):
            for hop in range(sections):
                signal(barrier, {axis: peer(axis, by), "section": peer("section", hop)})
    for hop in range(1, sections):
        signal(barrier, {"section": peer("section", hop)})
    greeted = sections * (groups + shards + experts - 2) - 1

    def token_copy(m):
        return pltpu.make_async_copy(tokens.at[m], held.at[m], tok_sem.at[m])

    for m in range(micro):
        token_copy(m).start()
    for a in range(3):
        pltpu.make_async_copy(sources[a], weights.at[a, me_s], own_sem).start()

    meta_own = pltpu.make_async_copy(meta_here, meta_v.at[me_s], meta_own_sem)

    def hand_back(m):
        return remote(
            held.at[m], out.at[m], hand_sem.at[0, m], hand_sem.at[1, m],
            {"section": peer("section", sections - 1)},
        )

    def comb_copy():
        return remote(
            comb, comb_in, comb_sem.at[0], comb_sem.at[1], {"section": peer("section", 1)}
        )

    def spot(group, k, shard):
        return weights.at[:, shard, pl.ds(group * half + cuts[k][0], cuts[k][1])]

    def staged(k, shard):
        if k == len(cuts):
            return stage.at[:, shard, pl.ds(keep, groups * extra)]
        return stage.at[:, shard, pl.ds(*cuts[k])]

    def origin(by):
        return peer("shard", shards - by)

    def outgoing(k):
        if k == len(cuts):
            return [(q * half + keep, keep + q * extra, extra) for q in range(groups)]
        return [(me_g * half + cuts[k][0], cuts[k][0], cuts[k][1])]

    relayed = [(k, by) for k in range(len(cuts)) for by in range(1, shards)]
    pairs = [(k, by) for k in range(pieces_in) for by in range(1, shards)]

    def start_stage():
        for k, by in pairs:
            for c, to, size in outgoing(k):
                remote(
                    weights.at[:, me_s, pl.ds(c, size)], stage.at[:, me_s, pl.ds(to, size)],
                    sx_send, sx_recv.at[k, by - 1],
                    {"shard": peer("shard", by), "section": peer("section", 1)},
                ).start()

    def stage_in(k, by):
        at = staged(k, origin(by))
        return remote(at, at, sx_send, sx_recv.at[k, by - 1], {"section": peer("section", 1)})

    def start_down(k, by):
        for c, to, size in outgoing(k):
            remote(
                stage.at[:, origin(by), pl.ds(to, size)],
                weights.at[:, origin(by), pl.ds(c, size)], sc_send, sc_recv.at[k, by - 1],
                {"section": peer("section", 1)},
            ).start()

    def stage_down(k, by):
        at = staged(k, origin(by))
        return remote(at, at, sc_send, sc_recv.at[k, by - 1], {"section": peer("section", 1)})

    def stage_over(k, by, hop, from_g):
        return remote(
            staged(k, origin(by)), spot(from_g, k, origin(by)), sy_send.at[hop - 1],
            sy_recv.at[k, by - 1, hop - 1],
            {"groups": peer("groups", hop), "section": peer("section", 1)},
        )

    def start_weights():
        for k, by in pairs:
            for c, to, size in outgoing(k):
                at = weights.at[:, me_s, pl.ds(c, size)]
                remote(
                    at, at, wx_send, wx_recv.at[k, by - 1], {"shard": peer("shard", by)}
                ).start()

    def weights_in(k, by):
        at = staged(k, origin(by))
        return remote(at, at, wx_send, wx_recv.at[k, by - 1], {"shard": peer("shard", by)})

    def weights_over(k, by, hop, from_g):
        at = spot(from_g, k, origin(by))
        return remote(
            at, at, wy_send.at[hop - 1], wy_recv.at[k, by - 1, hop - 1],
            {"groups": peer("groups", hop)},
        )

    def all_sent(sem, size=None):
        at = stage.at[:, pl.ds(0, shards - 1), pl.ds(0, size or keep + groups * extra)]
        remote(at, at, sem, wx_recv.at[0, 0], {"shard": peer("shard", 1)}).wait_send()

    def meta_over_shard(by):
        return remote(
            meta_here, meta_v.at[me_s], meta_send_sem.at[by - 1], meta_recv_sem.at[by - 1],
            {"shard": peer("shard", by)},
        )

    def relay_weights(begin, end):
        for k, by in pairs:
            if begin <= k < end:
                weights_in(k, by).wait_recv()
                if k < len(cuts):
                    for hop in range(1, groups):
                        weights_over(k, by, hop, me_g).start()

    def finish_relay(at):
        for k, by in relayed:
            if k == at:
                for hop in range(1, groups):
                    weights_over(k, by, hop, peer("groups", groups - hop)).wait_recv()

    def finish_stage(at):
        for k, by in pairs:
            if k == at:
                stage_down(k, by).wait_recv()
                if k < len(cuts):
                    for hop in range(1, groups):
                        stage_over(k, by, hop, peer("groups", groups - hop)).wait_recv()

    far_first = sorted(range(1, experts), key=lambda by: (abs(by - experts // 2), -by))

    def chunk_out(m, by):
        e = peer("expert", by)
        return remote(
            send.at[m, e], recv[m].at[me_e], disp_send.at[m], disp_recv.at[m], {"expert": e}
        )

    def chunk_self(m):
        return pltpu.make_async_copy(send.at[m, me_e], recv[m].at[me_e], disp_self.at[m])

    def chunks_far(m):
        return remote(
            send.at[m, pl.ds(0, experts - 1)], recv[m].at[pl.ds(0, experts - 1)],
            disp_send.at[m], disp_recv.at[m], {"expert": peer("expert", 1)},
        )

    def back_on(m, by):
        e = peer("expert", by)
        return remote(
            ret_send.at[m, e], ret_recv.at[0, m, me_e], back_send.at[m], back_recv.at[0, m],
            {"expert": e, "section": peer("section", 1)},
        )

    def back_on_all(m):
        return remote(
            ret_send.at[m], ret_recv.at[0, m], back_send.at[m], back_recv.at[0, m],
            {"section": peer("section", 1)},
        )

    def back_home(m, by):
        e = peer("expert", by)
        return remote(
            ret_send.at[m, e], ret_recv.at[1, m, me_e], back_send.at[m], back_recv.at[1, m],
            {"expert": e},
        )

    def back_far(m):
        return remote(
            ret_send.at[m, pl.ds(0, experts - 1)], ret_recv.at[1, m, pl.ds(0, experts - 1)],
            back_send.at[m], back_recv.at[1, m], {"expert": peer("expert", 1)},
        )

    def back_own(m):
        return pltpu.make_async_copy(
            ret_send.at[m, me_e], ret_recv.at[1, m, me_e], back_self.at[m]
        )

    def lanes(r):
        return pl.ds(pl.multiple_of(r * blk, blk), blk)

    def tail_line(e, j):
        return pl.ds(e * tail + j, blocks, stride=tails_all)

    def tail_part(j):
        return pl.ds(blocks + j * folds, folds)

    def put(dst, r, values):
        for e in range(experts):
            dst(e)[r] = values[e * main:(e + 1) * main].astype(BF16)
        tails_by[r] = values[experts * main:]

    def spread_tails(dst, e):
        for j in range(tail):
            lines = tails[tail_line(e, j), :].astype(BF16)
            dst(e)[tail_part(j)] = lines.reshape(folds, main, blk)

    def collect_tails(src):
        for e in range(experts):
            for j in range(tail):
                lines = src(e)[tail_part(j)].reshape(blocks, blk)
                tails[tail_line(e, j), :] = lines.astype(F32)

    def take(src, r):
        pieces_of = [src(e)[r] for e in range(experts)]
        return jnp.concatenate(pieces_of + [tails_by[r].astype(BF16)], axis=0)

    def dispatch(m):
        values = held[m].astype(F32)
        scale = lax.rsqrt(jnp.mean(values * values, axis=-1, keepdims=True) + EPS)
        normed[...] = (values * scale * gain[...]).astype(BF16)

        @pl.loop(0, blocks, unroll=8)
        def _(r):
            put(
                lambda e: send.at[m, e], r,
                jnp.dot(disp[m], normed[:, lanes(r)], preferred_element_type=F32),
            )

        for e in range(experts):
            spread_tails(lambda e: send.at[m, e], e)

    def send_chunks(m):
        for by in far_first:
            chunk_out(m, by).start()
        chunk_self(m).start()

    def listed(k):
        if k == len(cuts):
            return [
                (group * half + keep + u, groups * keep + group * extra + u)
                for group in range(groups) for u in range(extra)
            ]
        start, size = cuts[k]
        return [
            (group * half + start + u, groups * start + group * size + u)
            for group in range(groups) for u in range(size)
        ]

    whole = [item for k in range(pieces_in) for item in listed(k)]

    def segments(m, s, items):
        for i in range(0, len(items), RUN):
            segment(m, s, items[i:i + RUN])

    def segment(m, s, items):
        products = []
        for c, at in items:
            x = take(lambda e: recv[m].at[e], meta_s[s, 0, c])
            gate = jnp.dot(x, weights[0, s, c], preferred_element_type=F32)
            up = jnp.dot(x, weights[1, s, c], preferred_element_type=F32)
            hidden = (gate / (1.0 + jnp.exp(-gate)) * up).astype(BF16)
            product = jnp.dot(hidden, weights[2, s, c], preferred_element_type=F32)
            products.append((at, c, product))
        for at, c, product in products:
            parts[s, at] = product + parts[s, meta_s[s, 1, c]]

    def expert_part(m, opening):
        chunk_self(m).wait()
        chunks_far(m).wait()
        collect_tails(lambda e: recv[m].at[e])
        if opening:
            for by in range(1, shards):
                meta_over_shard(by).wait()
            meta_own.wait()
            load = pltpu.make_async_copy(meta_v, meta_s, meta_copy_sem)
            load.start()
            load.wait()
            segments(m, me_s, whole)
            for k in range(pieces_in):
                @pl.when(first)
                def _():
                    finish_stage(k)

                @pl.when(me_l > 0)
                def _():
                    finish_relay(k)

                @pl.loop(1, shards)
                def _(by):
                    segments(m, peer("shard", shards - by), listed(k))
        else:
            @pl.loop(0, shards)
            def _(s):
                segments(m, s, whole)

        @pl.loop(0, blocks, unroll=4)
        def _(j):
            total = parts[0, meta_s[0, 2, j]]
            for s in range(1, shards):
                total = total + parts[s, meta_s[s, 2, j]]
            put(lambda e: ret_send.at[m, e], j, total)

        for e in range(experts):
            spread_tails(lambda e: ret_send.at[m, e], e)

        @pl.when(me_l < sections - 1)
        def _():
            for by in far_first + [0]:
                back_on(m, by).start()

        @pl.when(last)
        def _():
            for by in far_first:
                back_home(m, by).start()
            back_own(m).start()

    def combine(m, which, dst):
        collect_tails(lambda e: ret_recv.at[which, m, e])

        @pl.loop(0, blocks, unroll=8)
        def _(r):
            mixed = jnp.dot(
                pieces[which, m], take(lambda e: ret_recv.at[which, m, e], r),
                preferred_element_type=F32,
            )
            mixed = mixed[:rows] + mixed[rows:2 * rows] + mixed[2 * rows:]
            dst[m, :, lanes(r)] = (held[m, :, lanes(r)].astype(F32) + mixed).astype(BF16)

    def split(which, m, value):
        for i in range(3):
            piece = value.astype(BF16)
            pieces[which, m, i * rows:(i + 1) * rows, :] = piece
            value = value - piece.astype(F32)

    def arrival(c):
        group = sum((c >= g * half).astype(jnp.int32) for g in range(1, groups))
        within = c - group * half
        start = sum(
            (within >= cuts[k][0]).astype(jnp.int32) * cuts[k - 1][1] for k in range(1, len(cuts))
        )
        size = cuts[0][1] + sum(
            (within >= cuts[k][0]).astype(jnp.int32) * (cuts[k][1] - cuts[k - 1][1])
            for k in range(1, len(cuts))
        )
        early = (groups - 1) * start + group * size + within
        return jnp.where(within < keep, early, groups * keep + group * extra + within - keep)

    def iota(shape, axis):
        return lax.broadcasted_iota(jnp.int32, shape, axis)

    slot = iota((slots, rows), 0)
    inner = slot - experts * main
    head = inner < 0
    expert_main = sum((slot >= e * main).astype(jnp.int32) for e in range(1, experts))
    expert_tail = sum((inner >= e * tail).astype(jnp.int32) for e in range(1, experts + 1))
    expert = jnp.where(head, expert_main, expert_tail)
    place_in = jnp.where(head, slot - expert_main * main, main + inner - expert_tail * tail)
    place_in = place_in.astype(F32)
    earlier = (iota((rows, rows), 0) < iota((rows, rows), 1)).astype(F32).astype(BF16)
    for m in range(micro):
        named = [ids[m, j:j + 1, :] == expert for j in range(TOP)]
        hit = functools.reduce(jnp.logical_or, named)
        ahead = jnp.dot(
            hit.astype(F32).astype(BF16), earlier, preferred_element_type=F32
        )
        fits = hit & (ahead == place_in)
        amount = sum(jnp.where(named[j], mix[m, j:j + 1, :], 0.0) for j in range(TOP))
        disp[m] = fits.astype(F32).astype(BF16)
        comb[m] = jnp.transpose(jnp.where(fits, amount, 0.0))

    cols = cols_in[...]
    cols_down = jnp.transpose(jnp.broadcast_to(cols, (n_blk, n_blk)))
    from_place = arrival(iota((n_blk, n_blk), 0))
    chained = (cols_down == cols) & (from_place < arrival(iota((n_blk, n_blk), 1)))
    before = jnp.max(jnp.where(chained, from_place, -1), axis=0, keepdims=True)
    final = jnp.broadcast_to(cols_down[:, :1], (n_blk, blocks)) == iota((n_blk, blocks), 1)
    last_at = jnp.where(final, arrival(iota((n_blk, blocks), 0)), -1)
    last_at = jnp.max(last_at, axis=0, keepdims=True)
    meta_here[...] = jnp.zeros_like(meta_here)
    meta_here[0:1, 0:n_blk] = rows_in[...]
    meta_here[1:2, 0:n_blk] = jnp.where(before < 0, n_blk, before)
    meta_here[2:3, 0:blocks] = jnp.where(last_at < 0, n_blk, last_at)
    for s in range(shards):
        parts[s, n_blk] = jnp.zeros_like(parts[s, n_blk])

    for m in range(micro):
        token_copy(m).wait()

    @pl.when(first)
    def _():
        dispatch(0)

    @pl.when(last)
    def _():
        for m in range(micro):
            split(1, m, comb[m])

    mine = weights.at[:, me_s]
    pltpu.make_async_copy(mine, mine, own_sem).wait()
    pl.semaphore_wait(barrier, greeted)

    for by in range(1, shards):
        meta_over_shard(by).start()
    meta_own.start()

    @pl.when(first)
    def _():
        start_stage()
        send_chunks(0)

    @pl.when(me_l < sections - 1)
    def _():
        comb_copy().start()

    @pl.when(first)
    def _():
        for m in range(1, micro):
            dispatch(m)
            send_chunks(m)

    @pl.when(me_l > 0)
    def _():
        for k, by in pairs:
            stage_in(k, by).wait_recv()
            if k < len(cuts):
                for hop in range(1, groups):
                    stage_over(k, by, hop, me_g).start()
            start_down(k, by)
        start_weights()
        comb_copy().wait_recv()
        for m in range(micro):
            split(0, m, comb_in[m])
        for m in range(micro):
            if m == 0:
                relay_weights(0, pieces_in if micro == 1 else pieces_in - 2)
            if m == 1:
                relay_weights(max(0, pieces_in - 2), pieces_in)
            back_on_all(m).wait_recv()
            if m > 0:
                send_chunks(m - 1)
            combine(m, 0, held)
            hand_back(m).start()
            dispatch(m)
        send_chunks(micro - 1)

    for m in range(micro):
        expert_part(m, m == 0)

    @pl.when(last)
    def _():
        for m in range(micro):
            back_own(m).wait()
            back_far(m).wait()
            combine(m, 1, out)

    @pl.when(me_l > 0)
    def _():
        for m in range(micro):
            hand_back(m).wait_send()
        all_sent(wx_send)
        all_sent(sc_send)
        for hop in range(1, groups):
            all_sent(sy_send.at[hop - 1], keep)
            all_sent(wy_send.at[hop - 1], keep)

    @pl.when(me_l < sections - 1)
    def _():
        comb_copy().wait_send()
        all_sent(sx_send)
        for m in range(micro):
            back_on_all(m).wait_send()
            hand_back(m).wait_recv()


def body(
    sizes,
    tokens,
    norm_gain,
    route_ids,
    route_weights,
    gate_blocks,
    up_blocks,
    down_blocks,
    gate_rows,
    down_cols,
):
    groups, shards, experts, sections = sizes
    assert sections == 2
    micro, rows, width = tokens.shape
    n_blk, blk = gate_blocks.shape[2], gate_blocks.shape[-1]
    blocks = width // blk
    cap = min(rows, max(rows * 9 // 16, rows * TOP // experts + 2))
    main = cap // 16 * 16
    tails_all = -(-(experts * (cap - main)) // 8) * 8
    slots = experts * main + tails_all

    extra = both_ways(n_blk // groups, groups)
    keep = n_blk // groups - extra
    cuts = len(cut_list(keep)) + min(extra, 1)
    meta_width = -(-max(n_blk, blocks) // 128) * 128
    dims = (micro, rows, blocks, blk, cap, experts, shards, groups, sections, n_blk)
    dma = pltpu.SemaphoreType.DMA
    assert blocks % main == 0
    chunk = (micro, experts, cap * blocks // main, main, blk)
    vmem, anywhere = pl.BlockSpec(memory_space=pltpu.VMEM), pl.BlockSpec(memory_space=pltpu.HBM)
    out = pl.pallas_call(
        functools.partial(layer_kernel, dims),
        out_shape=pltpu.VMEM((micro, rows, width), BF16),
        in_specs=[anywhere] + [vmem] * 3 + [anywhere] * 3 + [vmem] * 2,
        out_specs=vmem,
        scratch_shapes=[
            pltpu.VMEM((micro, rows, width), BF16),
            pltpu.VMEM((micro, slots, rows), BF16),
            pltpu.VMEM((micro, rows, slots), F32),
            pltpu.VMEM((micro, rows, slots), F32),
            pltpu.VMEM((2, micro, 3 * rows, slots), BF16),
            pltpu.VMEM((8, meta_width), jnp.int32),
            pltpu.VMEM((rows, width), BF16),
            pltpu.VMEM((tails_all * blocks, blk), F32),
            pltpu.VMEM(chunk, BF16),
            [pltpu.VMEM(chunk[1:], BF16) for _ in range(micro)],
            pltpu.VMEM((shards, n_blk + 1, slots, blk), F32),
            pltpu.VMEM(chunk, BF16),
            pltpu.VMEM((2,) + chunk, BF16),
            pltpu.VMEM((3, shards, n_blk, blk, blk), BF16),
            pltpu.VMEM((3, shards, keep + groups * extra, blk, blk), BF16),
            pltpu.VMEM((shards, 8, meta_width), jnp.int32),
            pltpu.SMEM((shards, 8, meta_width), jnp.int32),
            dma((micro,)),
            dma((2, micro)),
            dma,
            dma,
            dma((shards - 1,)),
            dma((shards - 1,)),
            dma,
            dma((2,)),
            dma,
            dma((cuts, shards - 1)),
            dma((groups - 1,)),
            dma((cuts, shards - 1, groups - 1)),
            dma((micro,)),
            dma((micro,)),
            dma((micro,)),
            dma((micro,)),
            dma((2, micro)),
            dma((micro,)),
            dma,
            dma((cuts, shards - 1)),
            dma,
            dma((cuts, shards - 1)),
            dma((groups - 1,)),
            dma((cuts, shards - 1, groups - 1)),
        ],
        compiler_params=pltpu.CompilerParams(
            collective_id=0, has_side_effects=True, vmem_limit_bytes=56 * 1024 * 1024
        ),
    )(
        tokens, norm_gain, jnp.swapaxes(route_ids[0], 1, 2), jnp.swapaxes(route_weights[0], 1, 2),
        gate_blocks.reshape(n_blk, blk, blk), up_blocks.reshape(n_blk, blk, blk),
        down_blocks.reshape(n_blk, blk, blk), gate_rows.reshape(1, n_blk),
        down_cols.reshape(1, n_blk),
    )
    return out[None]


def solution(mesh):
    sizes = tuple(mesh.shape[name] for name in ("groups", "shard", "expert", "section"))
    in_specs = (
        P(None, ("groups", "shard", "expert"), None),
        P("section", None),
        P("section", None, ("groups", "shard", "expert"), None),
        P("section", None, ("groups", "shard", "expert"), None),
        P("section", "expert", "shard", None, None, None),
        P("section", "expert", "shard", None, None, None),
        P("section", "expert", "shard", None, None, None),
        P("section", "expert", "shard", None),
        P("section", "expert", "shard", None),
    )
    out_specs = P("section", None, ("groups", "shard", "expert"), None)
    return jax.shard_map(
        functools.partial(body, sizes), mesh=mesh, in_specs=in_specs, out_specs=out_specs,
        check_vma=False,
    )
```

```python
import functools
import math

import jax
import jax.numpy as jnp
from jax import lax
from jax.experimental import pallas as pl
from jax.experimental.pallas import tpu as pltpu
from jax.sharding import PartitionSpec as P

TOP = 2
EPS = 1e-05
BF16 = jnp.bfloat16
F32 = jnp.float32
MOST = 2
RUN = 8


def both_ways(half, groups):
    return half // 8 if groups > 1 else 0


def cut_list(keep):
    cuts, at = [], 0
    while at < keep:
        size = min(MOST, at + 1, (keep - at + 1) // 2)
        cuts.append((at, size))
        at += size
    return cuts


def layer_kernel(
    dims,
    tokens, gain, ids, mix, gate_hbm, up_hbm, down_hbm, rows_in, cols_in,
    out,
    held, disp, comb, comb_in, pieces, meta_here, normed, tails, send, recv, parts, ret_send, ret_recv,
    weights, stage, meta_v, meta_s,
    tok_sem, hand_sem, own_sem, meta_own_sem, meta_send_sem, meta_recv_sem, meta_copy_sem, comb_sem,
    wx_send, wx_recv, wy_send, wy_recv, disp_send, disp_recv, disp_self,
    back_send, back_recv, back_self, sx_send, sx_recv, sc_send, sy_send,
):
    micro, rows, blocks, blk, cap, experts, shards, groups, sections, n_blk = dims
    main = cap // 16 * 16
    tail = cap - main
    tails_all = -(-(experts * tail) // 8) * 8
    slots = experts * main + tails_all
    folds = blocks // main
    tails_by = tails.reshape(blocks, tails_all, blk)
    me_g, me_s = lax.axis_index("groups"), lax.axis_index("shard")
    me_e, me_l = lax.axis_index("expert"), lax.axis_index("section")
    sizes = {"groups": groups, "shard": shards, "expert": experts, "section": sections}
    place = {"groups": me_g, "shard": me_s, "expert": me_e, "section": me_l}
    half = n_blk // groups
    extra = both_ways(half, groups)
    keep = half - extra
    cuts = cut_list(keep)
    sources = (gate_hbm, up_hbm, down_hbm)
    pieces_in = len(cuts) + min(extra, 1)
    first, last = me_l == 0, me_l == sections - 1

    def remote(src, dst, ssem, rsem, device):
        return pltpu.make_async_remote_copy(
            src_ref=src, dst_ref=dst, send_sem=ssem, recv_sem=rsem,
            device_id=device, device_id_type=pl.DeviceIdType.MESH,
        )

    def peer(axis, by):
        return lax.rem(place[axis] + by, sizes[axis])

    def signal(sem, device):
        pl.semaphore_signal(sem, inc=1, device_id=device, device_id_type=pl.DeviceIdType.MESH)

    barrier = pltpu.get_barrier_semaphore()
    for axis in ("expert", "shard", "groups"):
        for by in range(sizes[axis] - 1, 0, -1):
            for hop in range(sections):
                signal(barrier, {axis: peer(axis, by), "section": peer("section", hop)})
    for hop in range(1, sections):
        signal(barrier, {"section": peer("section", hop)})
    greeted = sections * (groups + shards + experts - 2) - 1

    def token_copy(m):
        return pltpu.make_async_copy(tokens.at[m], held.at[m], tok_sem.at[m])

    for m in range(micro):
        token_copy(m).start()
    for a in range(3):
        pltpu.make_async_copy(sources[a], weights.at[a, me_s], own_sem).start()

    meta_own = pltpu.make_async_copy(meta_here, meta_v.at[me_s], meta_own_sem)

    def hand_back(m):
        return remote(
            held.at[m], out.at[m], hand_sem.at[0, m], hand_sem.at[1, m],
            {"section": peer("section", sections - 1)},
        )

    def comb_copy():
        return remote(
            comb, comb_in, comb_sem.at[0], comb_sem.at[1], {"section": peer("section", 1)}
        )

    def spot(group, k, shard):
        return weights.at[:, shard, pl.ds(group * half + cuts[k][0], cuts[k][1])]

    def staged(k, shard):
        if k == len(cuts):
            return stage.at[:, shard, pl.ds(keep, groups * extra)]
        return stage.at[:, shard, pl.ds(*cuts[k])]

    def origin(by):
        return peer("shard", shards - by)

    def outgoing(k):
        if k == len(cuts):
            return [(q * half + keep, keep + q * extra, extra) for q in range(groups)]
        return [(me_g * half + cuts[k][0], cuts[k][0], cuts[k][1])]

    relayed = [(k, by) for k in range(len(cuts)) for by in range(1, shards)]
    pairs = [(k, by) for k in range(pieces_in) for by in range(1, shards)]

    def start_stage():
        for k, by in pairs:
            for c, to, size in outgoing(k):
                remote(
                    weights.at[:, me_s, pl.ds(c, size)], stage.at[:, me_s, pl.ds(to, size)],
                    sx_send, sx_recv.at[k, by - 1],
                    {"shard": peer("shard", by), "section": peer("section", 1)},
                ).start()

    def stage_in(k, by):
        at = staged(k, origin(by))
        return remote(at, at, sx_send, sx_recv.at[k, by - 1], {"section": peer("section", 1)})

    def start_down(k, by):
        for c, to, size in outgoing(k):
            remote(
                stage.at[:, origin(by), pl.ds(to, size)],
                weights.at[:, origin(by), pl.ds(c, size)], sc_send, wx_recv.at[k, by - 1],
                {"section": peer("section", 1)},
            ).start()

    def stage_down(k, by):
        at = staged(k, origin(by))
        return remote(at, at, sc_send, wx_recv.at[k, by - 1], {"section": peer("section", 1)})

    def stage_over(k, by, hop, from_g):
        return remote(
            staged(k, origin(by)), spot(from_g, k, origin(by)), sy_send.at[hop - 1],
            wy_recv.at[k, by - 1, hop - 1],
            {"groups": peer("groups", hop), "section": peer("section", 1)},
        )

    def start_weights():
        for k, by in pairs:
            for c, to, size in outgoing(k):
                at = weights.at[:, me_s, pl.ds(c, size)]
                remote(
                    at, at, wx_send, wx_recv.at[k, by - 1], {"shard": peer("shard", by)}
                ).start()

    def weights_in(k, by):
        at = staged(k, origin(by))
        return remote(at, at, wx_send, wx_recv.at[k, by - 1], {"shard": peer("shard", by)})

    def weights_over(k, by, hop, from_g):
        at = spot(from_g, k, origin(by))
        return remote(
            at, at, wy_send.at[hop - 1], wy_recv.at[k, by - 1, hop - 1],
            {"groups": peer("groups", hop)},
        )

    def all_sent(sem, size=None):
        at = stage.at[:, pl.ds(0, shards - 1), pl.ds(0, size or keep + groups * extra)]
        remote(at, at, sem, wx_recv.at[0, 0], {"shard": peer("shard", 1)}).wait_send()

    def meta_over_shard(by):
        return remote(
            meta_here, meta_v.at[me_s], meta_send_sem.at[by - 1], meta_recv_sem.at[by - 1],
            {"shard": peer("shard", by)},
        )

    def relay_weights(begin, end):
        for k, by in pairs:
            if begin <= k < end:
                weights_in(k, by).wait_recv()
                if k < len(cuts):
                    for hop in range(1, groups):
                        weights_over(k, by, hop, me_g).start()

    def finish_relay(at):
        for k, by in relayed:
            if k == at:
                for hop in range(1, groups):
                    weights_over(k, by, hop, peer("groups", groups - hop)).wait_recv()

    def finish_stage(at):
        for k, by in pairs:
            if k == at:
                stage_down(k, by).wait_recv()
                if k < len(cuts):
                    for hop in range(1, groups):
                        stage_over(k, by, hop, peer("groups", groups - hop)).wait_recv()

    far_first = sorted(range(1, experts), key=lambda by: (abs(by - experts // 2), -by))

    def chunk_out(m, by):
        e = peer("expert", by)
        return remote(
            send.at[m, e], recv[m].at[me_e], disp_send.at[m], disp_recv.at[m], {"expert": e}
        )

    def chunk_self(m):
        return pltpu.make_async_copy(send.at[m, me_e], recv[m].at[me_e], disp_self.at[m])

    def chunks_far(m):
        return remote(
            send.at[m, pl.ds(0, experts - 1)], recv[m].at[pl.ds(0, experts - 1)],
            disp_send.at[m], disp_recv.at[m], {"expert": peer("expert", 1)},
        )

    def back_on(m, by):
        e = peer("expert", by)
        return remote(
            ret_send.at[m, e], ret_recv.at[0, m, me_e], back_send.at[m], back_recv.at[0, m],
            {"expert": e, "section": peer("section", 1)},
        )

    def back_on_all(m):
        return remote(
            ret_send.at[m], ret_recv.at[0, m], back_send.at[m], back_recv.at[0, m],
            {"section": peer("section", 1)},
        )

    def back_home(m, by):
        e = peer("expert", by)
        return remote(
            ret_send.at[m, e], ret_recv.at[1, m, me_e], back_send.at[m], back_recv.at[1, m],
            {"expert": e},
        )

    def back_far(m):
        return remote(
            ret_send.at[m, pl.ds(0, experts - 1)], ret_recv.at[1, m, pl.ds(0, experts - 1)],
            back_send.at[m], back_recv.at[1, m], {"expert": peer("expert", 1)},
        )

    def back_own(m):
        return pltpu.make_async_copy(
            ret_send.at[m, me_e], ret_recv.at[1, m, me_e], back_self.at[m]
        )

    wide = 2 - blocks % 2

    def lanes(i):
        return pl.ds(pl.multiple_of(i * wide * blk, wide * blk), wide * blk)

    def tail_line(e, j):
        return pl.ds(e * tail + j, blocks, stride=tails_all)

    def tail_part(j):
        return pl.ds(blocks + j * folds, folds)

    def put(dst, r, values):
        for e in range(experts):
            dst(e)[r] = values[e * main:(e + 1) * main].astype(BF16)
        tails_by[r] = values[experts * main:]

    def spread_tails(dst, e):
        for j in range(tail):
            lines = tails[tail_line(e, j), :].astype(BF16)
            dst(e)[tail_part(j)] = lines.reshape(folds, main, blk)

    def collect_tails(src):
        for e in range(experts):
            for j in range(tail):
                lines = src(e)[tail_part(j)].reshape(blocks, blk)
                tails[tail_line(e, j), :] = lines.astype(F32)

    def take(src, r):
        pieces_of = [src(e)[r] for e in range(experts)]
        return jnp.concatenate(pieces_of + [tails_by[r].astype(BF16)], axis=0)

    def dispatch(m):
        values = held[m].astype(F32)
        scale = lax.rsqrt(jnp.mean(values * values, axis=-1, keepdims=True) + EPS)
        normed[...] = (values * scale * gain[...]).astype(BF16)

        @pl.loop(0, blocks // wide, unroll=True)
        def _(i):
            values = jnp.dot(disp[m], normed[:, lanes(i)], preferred_element_type=F32)
            for j in range(wide):
                put(lambda e: send.at[m, e], i * wide + j, values[:, j * blk:(j + 1) * blk])

        for e in range(experts):
            spread_tails(lambda e: send.at[m, e], e)

    def send_chunks(m):
        for by in far_first:
            chunk_out(m, by).start()
        chunk_self(m).start()

    def listed(k):
        if k == len(cuts):
            return [
                (group * half + keep + u, groups * keep + group * extra + u)
                for group in range(groups) for u in range(extra)
            ]
        start, size = cuts[k]
        return [
            (group * half + start + u, groups * start + group * size + u)
            for group in range(groups) for u in range(size)
        ]

    whole = [item for k in range(pieces_in) for item in listed(k)]

    def segments(m, s, items):
        for i in range(0, len(items), RUN):
            segment(m, s, items[i:i + RUN])

    def segment(m, s, items):
        products = []
        for c, at in items:
            x = take(lambda e: recv[m].at[e], meta_s[s, 0, c])
            both = jnp.concatenate([weights[0, s, c], weights[1, s, c]], axis=1)
            both = jnp.dot(x, both, preferred_element_type=F32)
            gate, up = both[:, :blk], both[:, blk:]
            hidden = (gate / (1.0 + jnp.exp(-gate)) * up).astype(BF16)
            product = jnp.dot(hidden, weights[2, s, c], preferred_element_type=F32)
            products.append((at, c, product))
        for at, c, product in products:
            parts[s, at] = product + parts[s, meta_s[s, 1, c]]

    def expert_part(m, opening):
        chunk_self(m).wait()
        chunks_far(m).wait()
        collect_tails(lambda e: recv[m].at[e])
        if opening:
            for by in range(1, shards):
                meta_over_shard(by).wait()
            meta_own.wait()
            load = pltpu.make_async_copy(meta_v, meta_s, meta_copy_sem)
            load.start()
            load.wait()
            segments(m, me_s, whole)
            for k in range(pieces_in):
                @pl.when(first)
                def _():
                    finish_stage(k)

                @pl.when(me_l > 0)
                def _():
                    finish_relay(k)

                @pl.loop(1, shards)
                def _(by):
                    segments(m, peer("shard", shards - by), listed(k))
        else:
            @pl.loop(0, shards)
            def _(s):
                segments(m, s, whole)

        @pl.loop(0, blocks, unroll=True)
        def _(j):
            total = parts[0, meta_s[0, 2, j]]
            for s in range(1, shards):
                total = total + parts[s, meta_s[s, 2, j]]
            put(lambda e: ret_send.at[m, e], j, total)

        for e in range(experts):
            spread_tails(lambda e: ret_send.at[m, e], e)

        @pl.when(me_l < sections - 1)
        def _():
            for by in far_first + [0]:
                back_on(m, by).start()

        @pl.when(last)
        def _():
            for by in far_first:
                back_home(m, by).start()
            back_own(m).start()

    def combine(m, which, dst):
        collect_tails(lambda e: ret_recv.at[which, m, e])

        @pl.loop(0, blocks // wide, unroll=True)
        def _(i):
            values = jnp.concatenate(
                [take(lambda e: ret_recv.at[which, m, e], i * wide + j) for j in range(wide)],
                axis=1,
            )
            mixed = jnp.dot(pieces[which, m], values, preferred_element_type=F32)
            mixed = mixed[:rows] + mixed[rows:2 * rows] + mixed[2 * rows:]
            dst[m, :, lanes(i)] = (held[m, :, lanes(i)].astype(F32) + mixed).astype(BF16)

    def split(which, m, value):
        for i in range(3):
            piece = value.astype(BF16)
            pieces[which, m, i * rows:(i + 1) * rows, :] = piece
            value = value - piece.astype(F32)

    def arrival(c):
        group = sum((c >= g * half).astype(jnp.int32) for g in range(1, groups))
        within = c - group * half
        start = sum(
            (within >= cuts[k][0]).astype(jnp.int32) * cuts[k - 1][1] for k in range(1, len(cuts))
        )
        size = cuts[0][1] + sum(
            (within >= cuts[k][0]).astype(jnp.int32) * (cuts[k][1] - cuts[k - 1][1])
            for k in range(1, len(cuts))
        )
        early = (groups - 1) * start + group * size + within
        return jnp.where(within < keep, early, groups * keep + group * extra + within - keep)

    def iota(shape, axis):
        return lax.broadcasted_iota(jnp.int32, shape, axis)

    slot = iota((slots, rows), 0)
    inner = slot - experts * main
    head = inner < 0
    expert_main = sum((slot >= e * main).astype(jnp.int32) for e in range(1, experts))
    expert_tail = sum((inner >= e * tail).astype(jnp.int32) for e in range(1, experts + 1))
    expert = jnp.where(head, expert_main, expert_tail)
    place_in = jnp.where(head, slot - expert_main * main, main + inner - expert_tail * tail)
    place_in = place_in.astype(F32)
    earlier = (iota((rows, rows), 0) < iota((rows, rows), 1)).astype(F32).astype(BF16)
    for m in range(micro):
        named = [ids[m, j:j + 1, :] == expert for j in range(TOP)]
        hit = functools.reduce(jnp.logical_or, named)
        ahead = jnp.dot(
            hit.astype(F32).astype(BF16), earlier, preferred_element_type=F32
        )
        fits = hit & (ahead == place_in)
        amount = sum(jnp.where(named[j], mix[m, j:j + 1, :], 0.0) for j in range(TOP))
        disp[m] = fits.astype(F32).astype(BF16)
        comb[m] = jnp.transpose(jnp.where(fits, amount, 0.0))

    cols = cols_in[...]
    cols_down = jnp.transpose(jnp.broadcast_to(cols, (n_blk, n_blk)))
    from_place = arrival(iota((n_blk, n_blk), 0))
    chained = (cols_down == cols) & (from_place < arrival(iota((n_blk, n_blk), 1)))
    before = jnp.max(jnp.where(chained, from_place, -1), axis=0, keepdims=True)
    final = jnp.broadcast_to(cols_down[:, :1], (n_blk, blocks)) == iota((n_blk, blocks), 1)
    last_at = jnp.where(final, arrival(iota((n_blk, blocks), 0)), -1)
    last_at = jnp.max(last_at, axis=0, keepdims=True)
    meta_here[...] = jnp.zeros_like(meta_here)
    meta_here[0:1, 0:n_blk] = rows_in[...]
    meta_here[1:2, 0:n_blk] = jnp.where(before < 0, n_blk, before)
    meta_here[2:3, 0:blocks] = jnp.where(last_at < 0, n_blk, last_at)
    for s in range(shards):
        parts[s, n_blk] = jnp.zeros_like(parts[s, n_blk])

    for m in range(micro):
        token_copy(m).wait()

    @pl.when(first)
    def _():
        dispatch(0)

    @pl.when(last)
    def _():
        for m in range(micro):
            split(1, m, comb[m])

    mine = weights.at[:, me_s]
    pltpu.make_async_copy(mine, mine, own_sem).wait()
    pl.semaphore_wait(barrier, greeted)

    for by in range(1, shards):
        meta_over_shard(by).start()
    meta_own.start()

    @pl.when(first)
    def _():
        start_stage()
        send_chunks(0)

    @pl.when(me_l < sections - 1)
    def _():
        comb_copy().start()

    @pl.when(first)
    def _():
        for m in range(1, micro):
            dispatch(m)
            send_chunks(m)

    @pl.when(me_l > 0)
    def _():
        for k, by in pairs:
            stage_in(k, by).wait_recv()
            if k < len(cuts):
                for hop in range(1, groups):
                    stage_over(k, by, hop, me_g).start()
            start_down(k, by)
        start_weights()
        comb_copy().wait_recv()
        for m in range(micro):
            split(0, m, comb_in[m])
        for m in range(micro):
            if m == 0:
                relay_weights(0, pieces_in if micro == 1 else pieces_in - 2)
            if m == 1:
                relay_weights(max(0, pieces_in - 2), pieces_in)
            back_on_all(m).wait_recv()
            if m > 0:
                send_chunks(m - 1)
            combine(m, 0, held)
            hand_back(m).start()
            dispatch(m)
        send_chunks(micro - 1)

    for m in range(micro):
        expert_part(m, m == 0)

    @pl.when(last)
    def _():
        for m in range(micro):
            back_own(m).wait()
            back_far(m).wait()
            combine(m, 1, out)

    @pl.when(me_l > 0)
    def _():
        for m in range(micro):
            hand_back(m).wait_send()
        all_sent(wx_send)
        all_sent(sc_send)
        for hop in range(1, groups):
            all_sent(sy_send.at[hop - 1], keep)
            all_sent(wy_send.at[hop - 1], keep)

    @pl.when(me_l < sections - 1)
    def _():
        comb_copy().wait_send()
        all_sent(sx_send)
        for m in range(micro):
            back_on_all(m).wait_send()
            hand_back(m).wait_recv()


def body(
    sizes,
    tokens,
    norm_gain,
    route_ids,
    route_weights,
    gate_blocks,
    up_blocks,
    down_blocks,
    gate_rows,
    down_cols,
):
    groups, shards, experts, sections = sizes
    assert sections == 2
    micro, rows, width = tokens.shape
    n_blk, blk = gate_blocks.shape[2], gate_blocks.shape[-1]
    blocks = width // blk
    cap = min(rows, max(rows * 9 // 16, rows * TOP // experts + 2))
    main = cap // 16 * 16
    tails_all = -(-(experts * (cap - main)) // 8) * 8
    slots = experts * main + tails_all

    extra = both_ways(n_blk // groups, groups)
    keep = n_blk // groups - extra
    cuts = len(cut_list(keep)) + min(extra, 1)
    meta_width = -(-max(n_blk, blocks) // 128) * 128
    dims = (micro, rows, blocks, blk, cap, experts, shards, groups, sections, n_blk)
    dma = pltpu.SemaphoreType.DMA
    assert blocks % main == 0
    chunk = (micro, experts, cap * blocks // main, main, blk)
    vmem, anywhere = pl.BlockSpec(memory_space=pltpu.VMEM), pl.BlockSpec(memory_space=pltpu.HBM)
    out = pl.pallas_call(
        functools.partial(layer_kernel, dims),
        out_shape=pltpu.VMEM((micro, rows, width), BF16),
        in_specs=[anywhere] + [vmem] * 3 + [anywhere] * 3 + [vmem] * 2,
        out_specs=vmem,
        scratch_shapes=[
            pltpu.VMEM((micro, rows, width), BF16),
            pltpu.VMEM((micro, slots, rows), BF16),
            pltpu.VMEM((micro, rows, slots), F32),
            pltpu.VMEM((micro, rows, slots), F32),
            pltpu.VMEM((2, micro, 3 * rows, slots), BF16),
            pltpu.VMEM((8, meta_width), jnp.int32),
            pltpu.VMEM((rows, width), BF16),
            pltpu.VMEM((tails_all * blocks, blk), F32),
            pltpu.VMEM(chunk, BF16),
            [pltpu.VMEM(chunk[1:], BF16) for _ in range(micro)],
            pltpu.VMEM((shards, n_blk + 1, slots, blk), F32),
            pltpu.VMEM(chunk, BF16),
            pltpu.VMEM((2,) + chunk, BF16),
            pltpu.VMEM((3, shards, n_blk, blk, blk), BF16),
            pltpu.VMEM((3, shards, keep + groups * extra, blk, blk), BF16),
            pltpu.VMEM((shards, 8, meta_width), jnp.int32),
            pltpu.SMEM((shards, 8, meta_width), jnp.int32),
            dma((micro,)),
            dma((2, micro)),
            dma,
            dma,
            dma((shards - 1,)),
            dma((shards - 1,)),
            dma,
            dma((2,)),
            dma,
            dma((cuts, shards - 1)),
            dma((groups - 1,)),
            dma((cuts, shards - 1, groups - 1)),
            dma((micro,)),
            dma((micro,)),
            dma((micro,)),
            dma((micro,)),
            dma((2, micro)),
            dma((micro,)),
            dma,
            dma((cuts, shards - 1)),
            dma,
            dma((groups - 1,)),
        ],
        compiler_params=pltpu.CompilerParams(
            collective_id=0, has_side_effects=True, vmem_limit_bytes=56 * 1024 * 1024
        ),
    )(
        tokens, norm_gain, jnp.swapaxes(route_ids[0], 1, 2), jnp.swapaxes(route_weights[0], 1, 2),
        gate_blocks.reshape(n_blk, blk, blk), up_blocks.reshape(n_blk, blk, blk),
        down_blocks.reshape(n_blk, blk, blk), gate_rows.reshape(1, n_blk),
        down_cols.reshape(1, n_blk),
    )
    return out[None]


def solution(mesh):
    sizes = tuple(mesh.shape[name] for name in ("groups", "shard", "expert", "section"))
    in_specs = (
        P(None, ("groups", "shard", "expert"), None),
        P("section", None),
        P("section", None, ("groups", "shard", "expert"), None),
        P("section", None, ("groups", "shard", "expert"), None),
        P("section", "expert", "shard", None, None, None),
        P("section", "expert", "shard", None, None, None),
        P("section", "expert", "shard", None, None, None),
        P("section", "expert", "shard", None),
        P("section", "expert", "shard", None),
    )
    out_specs = P("section", None, ("groups", "shard", "expert"), None)
    return jax.shard_map(
        functools.partial(body, sizes), mesh=mesh, in_specs=in_specs, out_specs=out_specs,
        check_vma=False,
    )
```

```python
import functools
import math

import jax
import jax.numpy as jnp
from jax import lax
from jax.experimental import pallas as pl
from jax.experimental.pallas import tpu as pltpu
from jax.sharding import PartitionSpec as P

TOP = 2
EPS = 1e-05
BF16 = jnp.bfloat16
F32 = jnp.float32
MOST = 2
RUN = 8


def both_ways(half, groups):
    return half // 8 if groups > 1 else 0


def cut_list(keep):
    cuts, at = [], 0
    while at < keep:
        size = min(MOST, at + 1, (keep - at + 1) // 2)
        cuts.append((at, size))
        at += size
    return cuts


def layer_kernel(
    dims,
    tokens, gain, ids, mix, gate_hbm, up_hbm, down_hbm, rows_in, cols_in,
    out,
    held, disp, comb, comb_in, pieces, meta_here, normed, tails, send, recv, parts, ret_send, ret_recv,
    weights, stage, meta_v, meta_s,
    tok_sem, hand_sem, own_sem, meta_own_sem, meta_send_sem, meta_recv_sem, meta_copy_sem, comb_sem,
    wx_send, wx_recv, wy_send, wy_recv, disp_send, disp_recv, disp_self,
    back_send, back_recv, back_self, sx_send, sx_recv, sc_send, sy_send, go_sem,
):
    micro, rows, blocks, blk, cap, experts, shards, groups, sections, n_blk = dims
    main = cap // 16 * 16
    tail = cap - main
    tails_all = -(-(experts * tail) // 8) * 8
    slots = experts * main + tails_all
    folds = blocks // main
    tails_by = tails.reshape(blocks, tails_all, blk)
    me_g, me_s = lax.axis_index("groups"), lax.axis_index("shard")
    me_e, me_l = lax.axis_index("expert"), lax.axis_index("section")
    sizes = {"groups": groups, "shard": shards, "expert": experts, "section": sections}
    place = {"groups": me_g, "shard": me_s, "expert": me_e, "section": me_l}
    half = n_blk // groups
    extra = both_ways(half, groups)
    keep = half - extra
    cuts = cut_list(keep)
    sources = (gate_hbm, up_hbm, down_hbm)
    pieces_in = len(cuts) + min(extra, 1)
    first, last = me_l == 0, me_l == sections - 1

    def remote(src, dst, ssem, rsem, device):
        return pltpu.make_async_remote_copy(
            src_ref=src, dst_ref=dst, send_sem=ssem, recv_sem=rsem,
            device_id=device, device_id_type=pl.DeviceIdType.MESH,
        )

    def peer(axis, by):
        return lax.rem(place[axis] + by, sizes[axis])

    def signal(sem, device):
        pl.semaphore_signal(sem, inc=1, device_id=device, device_id_type=pl.DeviceIdType.MESH)

    barrier = pltpu.get_barrier_semaphore()
    for axis in ("expert", "shard", "groups"):
        for by in range(sizes[axis] - 1, 0, -1):
            for hop in range(sections):
                signal(barrier, {axis: peer(axis, by), "section": peer("section", hop)})
    for hop in range(1, sections):
        signal(barrier, {"section": peer("section", hop)})
    greeted = sections * (groups + shards + experts - 2) - 1

    def token_copy(m):
        return pltpu.make_async_copy(tokens.at[m], held.at[m], tok_sem.at[m])

    for m in range(micro):
        token_copy(m).start()
    for a in range(3):
        pltpu.make_async_copy(sources[a], weights.at[a, me_s], own_sem).start()

    meta_own = pltpu.make_async_copy(meta_here, meta_v.at[me_s], meta_own_sem)

    def hand_back(m):
        return remote(
            held.at[m], out.at[m], hand_sem.at[0, m], hand_sem.at[1, m],
            {"section": peer("section", sections - 1)},
        )

    def comb_copy():
        return remote(
            comb, comb_in, comb_sem.at[0], comb_sem.at[1], {"section": peer("section", 1)}
        )

    def spot(group, k, shard):
        return weights.at[:, shard, pl.ds(group * half + cuts[k][0], cuts[k][1])]

    def staged(k, shard):
        if k == len(cuts):
            return stage.at[:, shard, pl.ds(keep, groups * extra)]
        return stage.at[:, shard, pl.ds(*cuts[k])]

    def origin(by):
        return peer("shard", shards - by)

    def outgoing(k):
        if k == len(cuts):
            return [(q * half + keep, keep + q * extra, extra) for q in range(groups)]
        return [(me_g * half + cuts[k][0], cuts[k][0], cuts[k][1])]

    relayed = [(k, by) for k in range(len(cuts)) for by in range(1, shards)]
    pairs = [(k, by) for k in range(pieces_in) for by in range(1, shards)]

    def start_stage():
        for k, by in pairs:
            for c, to, size in outgoing(k):
                at = weights.at[:, me_s, pl.ds(c, size)]
                if k < len(cuts):
                    remote(
                        at, stage.at[:, me_s, pl.ds(to, size)], sx_send, sx_recv.at[k, by - 1],
                        {"shard": peer("shard", by), "section": peer("section", 1)},
                    ).start()
                else:
                    remote(
                        at, at, sx_send, wx_recv.at[k, by - 1], {"shard": peer("shard", by)}
                    ).start()

    def stage_in(k, by):
        at = staged(k, origin(by))
        return remote(at, at, sx_send, sx_recv.at[k, by - 1], {"section": peer("section", 1)})

    def start_down(k, by):
        for c, to, size in outgoing(k):
            remote(
                stage.at[:, origin(by), pl.ds(to, size)],
                weights.at[:, origin(by), pl.ds(c, size)], sc_send, wx_recv.at[k, by - 1],
                {"section": peer("section", 1)},
            ).start()

    def stage_down(k, by):
        at = staged(k, origin(by))
        return remote(at, at, sc_send, wx_recv.at[k, by - 1], {"section": peer("section", 1)})

    def stage_over(k, by, hop, from_g):
        return remote(
            staged(k, origin(by)), spot(from_g, k, origin(by)), sy_send.at[hop - 1],
            wy_recv.at[k, by - 1, hop - 1],
            {"groups": peer("groups", hop), "section": peer("section", 1)},
        )

    def start_weights():
        for k, by in pairs:
            for c, to, size in outgoing(k):
                at = weights.at[:, me_s, pl.ds(c, size)]
                remote(
                    at, at, wx_send, wx_recv.at[k, by - 1], {"shard": peer("shard", by)}
                ).start()

    def weights_in(k, by):
        at = staged(k, origin(by))
        return remote(at, at, wx_send, wx_recv.at[k, by - 1], {"shard": peer("shard", by)})

    def weights_over(k, by, hop, from_g):
        at = spot(from_g, k, origin(by))
        return remote(
            at, at, wy_send.at[hop - 1], wy_recv.at[k, by - 1, hop - 1],
            {"groups": peer("groups", hop)},
        )

    def all_sent(sem, size=None):
        at = stage.at[:, pl.ds(0, shards - 1), pl.ds(0, size or keep + groups * extra)]
        remote(at, at, sem, wx_recv.at[0, 0], {"shard": peer("shard", 1)}).wait_send()

    def meta_over_shard(by):
        return remote(
            meta_here, meta_v.at[me_s], meta_send_sem.at[by - 1], meta_recv_sem.at[by - 1],
            {"shard": peer("shard", by)},
        )

    def relay_weights(begin, end):
        for k, by in pairs:
            if begin <= k < end:
                weights_in(k, by).wait_recv()
                if k < len(cuts):
                    for hop in range(1, groups):
                        weights_over(k, by, hop, me_g).start()

    def finish_relay(at):
        for k, by in relayed:
            if k == at:
                for hop in range(1, groups):
                    weights_over(k, by, hop, peer("groups", groups - hop)).wait_recv()

    def finish_stage(at):
        for k, by in pairs:
            if k == at:
                stage_down(k, by).wait_recv()
                if k < len(cuts):
                    for hop in range(1, groups):
                        stage_over(k, by, hop, peer("groups", groups - hop)).wait_recv()

    far_first = sorted(range(1, experts), key=lambda by: (abs(by - experts // 2), -by))

    def chunk_out(m, by):
        e = peer("expert", by)
        return remote(
            send.at[m, e], recv[m].at[me_e], disp_send.at[m], disp_recv.at[m], {"expert": e}
        )

    def chunk_self(m):
        return pltpu.make_async_copy(send.at[m, me_e], recv[m].at[me_e], disp_self.at[m])

    def chunks_far(m):
        return remote(
            send.at[m, pl.ds(0, experts - 1)], recv[m].at[pl.ds(0, experts - 1)],
            disp_send.at[m], disp_recv.at[m], {"expert": peer("expert", 1)},
        )

    def back_on(m, by):
        e = peer("expert", by)
        return remote(
            ret_send.at[m, e], ret_recv.at[0, m, me_e], back_send.at[m], back_recv.at[0, m],
            {"expert": e, "section": peer("section", 1)},
        )

    def back_on_all(m):
        return remote(
            ret_send.at[m], ret_recv.at[0, m], back_send.at[m], back_recv.at[0, m],
            {"section": peer("section", 1)},
        )

    def back_home(m, by):
        e = peer("expert", by)
        return remote(
            ret_send.at[m, e], ret_recv.at[1, m, me_e], back_send.at[m], back_recv.at[1, m],
            {"expert": e},
        )

    def back_far(m):
        return remote(
            ret_send.at[m, pl.ds(0, experts - 1)], ret_recv.at[1, m, pl.ds(0, experts - 1)],
            back_send.at[m], back_recv.at[1, m], {"expert": peer("expert", 1)},
        )

    def back_own(m):
        return pltpu.make_async_copy(
            ret_send.at[m, me_e], ret_recv.at[1, m, me_e], back_self.at[m]
        )

    wide = 2 - blocks % 2

    def lanes(i):
        return pl.ds(pl.multiple_of(i * wide * blk, wide * blk), wide * blk)

    def tail_line(e, j):
        return pl.ds(e * tail + j, blocks, stride=tails_all)

    def tail_part(j):
        return pl.ds(blocks + j * folds, folds)

    def put(dst, r, values):
        for e in range(experts):
            dst(e)[r] = values[e * main:(e + 1) * main].astype(BF16)
        tails_by[r] = values[experts * main:]

    def spread_tails(dst, e):
        for j in range(tail):
            lines = tails[tail_line(e, j), :].astype(BF16)
            dst(e)[tail_part(j)] = lines.reshape(folds, main, blk)

    def collect_tails(src):
        for e in range(experts):
            for j in range(tail):
                lines = src(e)[tail_part(j)].reshape(blocks, blk)
                tails[tail_line(e, j), :] = lines.astype(F32)

    def take(src, r):
        pieces_of = [src(e)[r] for e in range(experts)]
        return jnp.concatenate(pieces_of + [tails_by[r].astype(BF16)], axis=0)

    def dispatch(m):
        values = held[m].astype(F32)
        scale = lax.rsqrt(jnp.mean(values * values, axis=-1, keepdims=True) + EPS)
        normed[...] = (values * scale * gain[...]).astype(BF16)

        @pl.loop(0, blocks // wide, unroll=True)
        def _(i):
            values = jnp.dot(disp[m], normed[:, lanes(i)], preferred_element_type=F32)
            for j in range(wide):
                put(lambda e: send.at[m, e], i * wide + j, values[:, j * blk:(j + 1) * blk])

        for e in range(experts):
            spread_tails(lambda e: send.at[m, e], e)

    def send_chunks(m):
        for by in far_first:
            chunk_out(m, by).start()
        chunk_self(m).start()

    def listed(k):
        if k == len(cuts):
            return [
                (group * half + keep + u, groups * keep + group * extra + u)
                for group in range(groups) for u in range(extra)
            ]
        start, size = cuts[k]
        return [
            (group * half + start + u, groups * start + group * size + u)
            for group in range(groups) for u in range(size)
        ]

    whole = [item for k in range(pieces_in) for item in listed(k)]

    def segments(m, s, items):
        for i in range(0, len(items), RUN):
            segment(m, s, items[i:i + RUN])

    def segment(m, s, items):
        products = []
        for c, at in items:
            x = take(lambda e: recv[m].at[e], meta_s[s, 0, c])
            both = jnp.concatenate([weights[0, s, c], weights[1, s, c]], axis=1)
            both = jnp.dot(x, both, preferred_element_type=F32)
            gate, up = both[:, :blk], both[:, blk:]
            hidden = (gate / (1.0 + jnp.exp(-gate)) * up).astype(BF16)
            product = jnp.dot(hidden, weights[2, s, c], preferred_element_type=F32)
            products.append((at, c, product))
        for at, c, product in products:
            parts[s, at] = product + parts[s, meta_s[s, 1, c]]

    def expert_part(m, opening):
        chunk_self(m).wait()
        chunks_far(m).wait()
        collect_tails(lambda e: recv[m].at[e])
        if opening:
            for by in range(1, shards):
                meta_over_shard(by).wait()
            meta_own.wait()
            load = pltpu.make_async_copy(meta_v, meta_s, meta_copy_sem)
            load.start()
            load.wait()
            @pl.when(first)
            def _():
                segments(m, me_s, whole)
                for k in range(pieces_in):
                    finish_stage(k)
                    if k == pieces_in - 1:
                        signal(go_sem, {"section": peer("section", 1)})

                    @pl.loop(1, shards)
                    def _(by):
                        segments(m, peer("shard", shards - by), listed(k))

            @pl.when(me_l > 0)
            def _():
                for k in range(pieces_in):
                    finish_relay(k)

                @pl.loop(0, shards)
                def _(s):
                    segments(m, s, whole)
        else:
            @pl.loop(0, shards)
            def _(s):
                segments(m, s, whole)

        @pl.loop(0, blocks, unroll=True)
        def _(j):
            total = parts[0, meta_s[0, 2, j]]
            for s in range(1, shards):
                total = total + parts[s, meta_s[s, 2, j]]
            put(lambda e: ret_send.at[m, e], j, total)

        for e in range(experts):
            spread_tails(lambda e: ret_send.at[m, e], e)

        @pl.when(me_l < sections - 1)
        def _():
            for by in far_first + [0]:
                back_on(m, by).start()

        @pl.when(last)
        def _():
            for by in far_first:
                back_home(m, by).start()
            back_own(m).start()

    def combine(m, which, dst):
        collect_tails(lambda e: ret_recv.at[which, m, e])

        @pl.loop(0, blocks // wide, unroll=True)
        def _(i):
            values = jnp.concatenate(
                [take(lambda e: ret_recv.at[which, m, e], i * wide + j) for j in range(wide)],
                axis=1,
            )
            mixed = jnp.dot(pieces[which, m], values, preferred_element_type=F32)
            mixed = mixed[:rows] + mixed[rows:2 * rows] + mixed[2 * rows:]
            dst[m, :, lanes(i)] = (held[m, :, lanes(i)].astype(F32) + mixed).astype(BF16)

    def split(which, m, value):
        for i in range(3):
            piece = value.astype(BF16)
            pieces[which, m, i * rows:(i + 1) * rows, :] = piece
            value = value - piece.astype(F32)

    def arrival(c):
        group = sum((c >= g * half).astype(jnp.int32) for g in range(1, groups))
        within = c - group * half
        start = sum(
            (within >= cuts[k][0]).astype(jnp.int32) * cuts[k - 1][1] for k in range(1, len(cuts))
        )
        size = cuts[0][1] + sum(
            (within >= cuts[k][0]).astype(jnp.int32) * (cuts[k][1] - cuts[k - 1][1])
            for k in range(1, len(cuts))
        )
        early = (groups - 1) * start + group * size + within
        return jnp.where(within < keep, early, groups * keep + group * extra + within - keep)

    def iota(shape, axis):
        return lax.broadcasted_iota(jnp.int32, shape, axis)

    slot = iota((slots, rows), 0)
    inner = slot - experts * main
    head = inner < 0
    expert_main = sum((slot >= e * main).astype(jnp.int32) for e in range(1, experts))
    expert_tail = sum((inner >= e * tail).astype(jnp.int32) for e in range(1, experts + 1))
    expert = jnp.where(head, expert_main, expert_tail)
    place_in = jnp.where(head, slot - expert_main * main, main + inner - expert_tail * tail)
    place_in = place_in.astype(F32)
    earlier = (iota((rows, rows), 0) < iota((rows, rows), 1)).astype(F32).astype(BF16)
    for m in range(micro):
        named = [ids[m, j:j + 1, :] == expert for j in range(TOP)]
        hit = functools.reduce(jnp.logical_or, named)
        ahead = jnp.dot(
            hit.astype(F32).astype(BF16), earlier, preferred_element_type=F32
        )
        fits = hit & (ahead == place_in)
        amount = sum(jnp.where(named[j], mix[m, j:j + 1, :], 0.0) for j in range(TOP))
        disp[m] = fits.astype(F32).astype(BF16)
        comb[m] = jnp.transpose(jnp.where(fits, amount, 0.0))

    cols = cols_in[...]
    cols_down = jnp.transpose(jnp.broadcast_to(cols, (n_blk, n_blk)))
    from_place = arrival(iota((n_blk, n_blk), 0))
    chained = (cols_down == cols) & (from_place < arrival(iota((n_blk, n_blk), 1)))
    before = jnp.max(jnp.where(chained, from_place, -1), axis=0, keepdims=True)
    final = jnp.broadcast_to(cols_down[:, :1], (n_blk, blocks)) == iota((n_blk, blocks), 1)
    last_at = jnp.where(final, arrival(iota((n_blk, blocks), 0)), -1)
    last_at = jnp.max(last_at, axis=0, keepdims=True)
    meta_here[...] = jnp.zeros_like(meta_here)
    meta_here[0:1, 0:n_blk] = rows_in[...]
    meta_here[1:2, 0:n_blk] = jnp.where(before < 0, n_blk, before)
    meta_here[2:3, 0:blocks] = jnp.where(last_at < 0, n_blk, last_at)
    for s in range(shards):
        parts[s, n_blk] = jnp.zeros_like(parts[s, n_blk])

    for m in range(micro):
        token_copy(m).wait()

    @pl.when(first)
    def _():
        dispatch(0)

    @pl.when(last)
    def _():
        for m in range(micro):
            split(1, m, comb[m])

    mine = weights.at[:, me_s]
    pltpu.make_async_copy(mine, mine, own_sem).wait()
    pl.semaphore_wait(barrier, greeted)

    for by in range(1, shards):
        meta_over_shard(by).start()
    meta_own.start()

    @pl.when(first)
    def _():
        start_stage()
        send_chunks(0)

    @pl.when(me_l < sections - 1)
    def _():
        comb_copy().start()

    @pl.when(first)
    def _():
        for m in range(1, micro):
            dispatch(m)
            send_chunks(m)

    @pl.when(me_l > 0)
    def _():
        for k, by in relayed:
            stage_in(k, by).wait_recv()
            for hop in range(1, groups):
                stage_over(k, by, hop, me_g).start()
            start_down(k, by)
        comb_copy().wait_recv()
        for m in range(micro):
            split(0, m, comb_in[m])
        pl.semaphore_wait(go_sem, 1)
        start_weights()
        early = max(0, pieces_in - 4)
        for m in range(micro):
            if m == 0:
                relay_weights(0, early)
            back_on_all(m).wait_recv()
            if m > 0:
                send_chunks(m - 1)
            combine(m, 0, held)
            hand_back(m).start()
            dispatch(m)
        send_chunks(micro - 1)
        relay_weights(early, pieces_in)

    for m in range(micro):
        expert_part(m, m == 0)

    @pl.when(last)
    def _():
        for m in range(micro):
            back_own(m).wait()
            back_far(m).wait()
            combine(m, 1, out)

    @pl.when(me_l > 0)
    def _():
        for m in range(micro):
            hand_back(m).wait_send()
        all_sent(wx_send)
        all_sent(sc_send, keep)
        for hop in range(1, groups):
            all_sent(sy_send.at[hop - 1], keep)
            all_sent(wy_send.at[hop - 1], keep)

    @pl.when(me_l < sections - 1)
    def _():
        comb_copy().wait_send()
        all_sent(sx_send)
        for m in range(micro):
            back_on_all(m).wait_send()
            hand_back(m).wait_recv()


def body(
    sizes,
    tokens,
    norm_gain,
    route_ids,
    route_weights,
    gate_blocks,
    up_blocks,
    down_blocks,
    gate_rows,
    down_cols,
):
    groups, shards, experts, sections = sizes
    assert sections == 2
    micro, rows, width = tokens.shape
    n_blk, blk = gate_blocks.shape[2], gate_blocks.shape[-1]
    blocks = width // blk
    cap = min(rows, max(rows * 9 // 16, rows * TOP // experts + 2))
    main = cap // 16 * 16
    tails_all = -(-(experts * (cap - main)) // 8) * 8
    slots = experts * main + tails_all

    extra = both_ways(n_blk // groups, groups)
    keep = n_blk // groups - extra
    cuts = len(cut_list(keep)) + min(extra, 1)
    meta_width = -(-max(n_blk, blocks) // 128) * 128
    dims = (micro, rows, blocks, blk, cap, experts, shards, groups, sections, n_blk)
    dma = pltpu.SemaphoreType.DMA
    assert blocks % main == 0
    chunk = (micro, experts, cap * blocks // main, main, blk)
    vmem, anywhere = pl.BlockSpec(memory_space=pltpu.VMEM), pl.BlockSpec(memory_space=pltpu.HBM)
    out = pl.pallas_call(
        functools.partial(layer_kernel, dims),
        out_shape=pltpu.VMEM((micro, rows, width), BF16),
        in_specs=[anywhere] + [vmem] * 3 + [anywhere] * 3 + [vmem] * 2,
        out_specs=vmem,
        scratch_shapes=[
            pltpu.VMEM((micro, rows, width), BF16),
            pltpu.VMEM((micro, slots, rows), BF16),
            pltpu.VMEM((micro, rows, slots), F32),
            pltpu.VMEM((micro, rows, slots), F32),
            pltpu.VMEM((2, micro, 3 * rows, slots), BF16),
            pltpu.VMEM((8, meta_width), jnp.int32),
            pltpu.VMEM((rows, width), BF16),
            pltpu.VMEM((tails_all * blocks, blk), F32),
            pltpu.VMEM(chunk, BF16),
            [pltpu.VMEM(chunk[1:], BF16) for _ in range(micro)],
            pltpu.VMEM((shards, n_blk + 1, slots, blk), F32),
            pltpu.VMEM(chunk, BF16),
            pltpu.VMEM((2,) + chunk, BF16),
            pltpu.VMEM((3, shards, n_blk, blk, blk), BF16),
            pltpu.VMEM((3, shards, keep + groups * extra, blk, blk), BF16),
            pltpu.VMEM((shards, 8, meta_width), jnp.int32),
            pltpu.SMEM((shards, 8, meta_width), jnp.int32),
            dma((micro,)),
            dma((2, micro)),
            dma,
            dma,
            dma((shards - 1,)),
            dma((shards - 1,)),
            dma,
            dma((2,)),
            dma,
            dma((cuts, shards - 1)),
            dma((groups - 1,)),
            dma((cuts, shards - 1, groups - 1)),
            dma((micro,)),
            dma((micro,)),
            dma((micro,)),
            dma((micro,)),
            dma((2, micro)),
            dma((micro,)),
            dma,
            dma((cuts, shards - 1)),
            dma,
            dma((groups - 1,)),
            pltpu.SemaphoreType.REGULAR,
        ],
        compiler_params=pltpu.CompilerParams(
            collective_id=0, has_side_effects=True, vmem_limit_bytes=56 * 1024 * 1024
        ),
    )(
        tokens, norm_gain, jnp.swapaxes(route_ids[0], 1, 2), jnp.swapaxes(route_weights[0], 1, 2),
        gate_blocks.reshape(n_blk, blk, blk), up_blocks.reshape(n_blk, blk, blk),
        down_blocks.reshape(n_blk, blk, blk), gate_rows.reshape(1, n_blk),
        down_cols.reshape(1, n_blk),
    )
    return out[None]


def solution(mesh):
    sizes = tuple(mesh.shape[name] for name in ("groups", "shard", "expert", "section"))
    in_specs = (
        P(None, ("groups", "shard", "expert"), None),
        P("section", None),
        P("section", None, ("groups", "shard", "expert"), None),
        P("section", None, ("groups", "shard", "expert"), None),
        P("section", "expert", "shard", None, None, None),
        P("section", "expert", "shard", None, None, None),
        P("section", "expert", "shard", None, None, None),
        P("section", "expert", "shard", None),
        P("section", "expert", "shard", None),
    )
    out_specs = P("section", None, ("groups", "shard", "expert"), None)
    return jax.shard_map(
        functools.partial(body, sizes), mesh=mesh, in_specs=in_specs, out_specs=out_specs,
        check_vma=False,
    )
```

```python
import functools
import math

import jax
import jax.numpy as jnp
from jax import lax
from jax.experimental import pallas as pl
from jax.experimental.pallas import tpu as pltpu
from jax.sharding import PartitionSpec as P

TOP = 2
EPS = 1e-05
BF16 = jnp.bfloat16
F32 = jnp.float32
MOST = 2
RUN = 8


def both_ways(half, groups):
    return half // 8 if groups > 1 else 0


def cut_list(keep):
    cuts, at = [], 0
    while at < keep:
        size = min(MOST, at + 1, (keep - at + 1) // 2)
        cuts.append((at, size))
        at += size
    return cuts


def layer_kernel(
    dims,
    tokens, gain, ids, mix, gate_hbm, up_hbm, down_hbm, rows_in, cols_in,
    out,
    held, disp, comb, comb_in, pieces, meta_here, normed, tails, send, recv, parts, ret_send, ret_recv,
    weights, stage, meta_v, meta_s,
    tok_sem, hand_sem, own_sem, meta_own_sem, meta_send_sem, meta_recv_sem, meta_copy_sem, comb_sem,
    wx_send, wx_recv, wy_send, wy_recv, disp_send, disp_recv, disp_self,
    back_send, back_recv, back_self, sx_send, sx_recv, sc_send, sy_send, go_sem,
):
    micro, rows, blocks, blk, cap, experts, shards, groups, sections, n_blk = dims
    main = cap // 16 * 16
    tail = cap - main
    tails_all = -(-(experts * tail) // 8) * 8
    slots = experts * main + tails_all
    folds = blocks // main
    tails_by = tails.reshape(blocks, tails_all, blk)
    me_g, me_s = lax.axis_index("groups"), lax.axis_index("shard")
    me_e, me_l = lax.axis_index("expert"), lax.axis_index("section")
    sizes = {"groups": groups, "shard": shards, "expert": experts, "section": sections}
    place = {"groups": me_g, "shard": me_s, "expert": me_e, "section": me_l}
    half = n_blk // groups
    extra = both_ways(half, groups)
    keep = half - extra
    cuts = cut_list(keep)
    sources = (gate_hbm, up_hbm, down_hbm)
    pieces_in = len(cuts) + min(extra, 1)
    first, last = me_l == 0, me_l == sections - 1

    def remote(src, dst, ssem, rsem, device):
        return pltpu.make_async_remote_copy(
            src_ref=src, dst_ref=dst, send_sem=ssem, recv_sem=rsem,
            device_id=device, device_id_type=pl.DeviceIdType.MESH,
        )

    def peer(axis, by):
        return lax.rem(place[axis] + by, sizes[axis])

    def signal(sem, device):
        pl.semaphore_signal(sem, inc=1, device_id=device, device_id_type=pl.DeviceIdType.MESH)

    barrier = pltpu.get_barrier_semaphore()
    for axis in ("expert", "shard", "groups"):
        for by in range(sizes[axis] - 1, 0, -1):
            for hop in range(sections):
                signal(barrier, {axis: peer(axis, by), "section": peer("section", hop)})
    for hop in range(1, sections):
        signal(barrier, {"section": peer("section", hop)})
    greeted = sections * (groups + shards + experts - 2) - 1

    def token_copy(m):
        return pltpu.make_async_copy(tokens.at[m], held.at[m], tok_sem.at[m])

    for m in range(micro):
        token_copy(m).start()
    for a in range(3):
        pltpu.make_async_copy(sources[a], weights.at[a, me_s], own_sem).start()

    meta_own = pltpu.make_async_copy(meta_here, meta_v.at[me_s], meta_own_sem)

    def hand_back(m):
        return remote(
            held.at[m], out.at[m], hand_sem.at[0, m], hand_sem.at[1, m],
            {"section": peer("section", sections - 1)},
        )

    def comb_copy():
        return remote(
            comb, comb_in, comb_sem.at[0], comb_sem.at[1], {"section": peer("section", 1)}
        )

    def spot(group, k, shard):
        return weights.at[:, shard, pl.ds(group * half + cuts[k][0], cuts[k][1])]

    def staged(k, shard):
        if k == len(cuts):
            return stage.at[:, shard, pl.ds(keep, groups * extra)]
        return stage.at[:, shard, pl.ds(*cuts[k])]

    def origin(by):
        return peer("shard", shards - by)

    def outgoing(k):
        if k == len(cuts):
            return [(q * half + keep, keep + q * extra, extra) for q in range(groups)]
        return [(me_g * half + cuts[k][0], cuts[k][0], cuts[k][1])]

    relayed = [(k, by) for k in range(len(cuts)) for by in range(1, shards)]
    pairs = [(k, by) for k in range(pieces_in) for by in range(1, shards)]

    def start_stage():
        for k, by in pairs:
            for c, to, size in outgoing(k):
                at = weights.at[:, me_s, pl.ds(c, size)]
                if k < len(cuts):
                    remote(
                        at, stage.at[:, me_s, pl.ds(to, size)], sx_send, sx_recv.at[k, by - 1],
                        {"shard": peer("shard", by), "section": peer("section", 1)},
                    ).start()
                else:
                    remote(
                        at, at, sx_send, wx_recv.at[k, by - 1], {"shard": peer("shard", by)}
                    ).start()

    def stage_in(k, by):
        at = staged(k, origin(by))
        return remote(at, at, sx_send, sx_recv.at[k, by - 1], {"section": peer("section", 1)})

    def start_down(k, by):
        for c, to, size in outgoing(k):
            remote(
                stage.at[:, origin(by), pl.ds(to, size)],
                weights.at[:, origin(by), pl.ds(c, size)], sc_send, wx_recv.at[k, by - 1],
                {"section": peer("section", 1)},
            ).start()

    def stage_down(k, by):
        at = staged(k, origin(by))
        return remote(at, at, sc_send, wx_recv.at[k, by - 1], {"section": peer("section", 1)})

    def stage_over(k, by, hop, from_g):
        return remote(
            staged(k, origin(by)), spot(from_g, k, origin(by)), sy_send.at[hop - 1],
            wy_recv.at[k, by - 1, hop - 1],
            {"groups": peer("groups", hop), "section": peer("section", 1)},
        )

    def start_weights():
        for k, by in pairs:
            for c, to, size in outgoing(k):
                at = weights.at[:, me_s, pl.ds(c, size)]
                remote(
                    at, at, wx_send, wx_recv.at[k, by - 1], {"shard": peer("shard", by)}
                ).start()

    def weights_in(k, by):
        at = staged(k, origin(by))
        return remote(at, at, wx_send, wx_recv.at[k, by - 1], {"shard": peer("shard", by)})

    def weights_over(k, by, hop, from_g):
        at = spot(from_g, k, origin(by))
        return remote(
            at, at, wy_send.at[hop - 1], wy_recv.at[k, by - 1, hop - 1],
            {"groups": peer("groups", hop)},
        )

    def all_sent(sem, size=None):
        at = stage.at[:, pl.ds(0, shards - 1), pl.ds(0, size or keep + groups * extra)]
        remote(at, at, sem, wx_recv.at[0, 0], {"shard": peer("shard", 1)}).wait_send()

    def meta_over_shard(by):
        return remote(
            meta_here, meta_v.at[me_s], meta_send_sem.at[by - 1], meta_recv_sem.at[by - 1],
            {"shard": peer("shard", by)},
        )

    def relay_weights(begin, end):
        for k, by in pairs:
            if begin <= k < end:
                weights_in(k, by).wait_recv()
                if k < len(cuts):
                    for hop in range(1, groups):
                        weights_over(k, by, hop, me_g).start()

    def finish_relay(at):
        for k, by in relayed:
            if k == at:
                for hop in range(1, groups):
                    weights_over(k, by, hop, peer("groups", groups - hop)).wait_recv()

    def finish_stage(at):
        for k, by in pairs:
            if k == at:
                stage_down(k, by).wait_recv()
                if k < len(cuts):
                    for hop in range(1, groups):
                        stage_over(k, by, hop, peer("groups", groups - hop)).wait_recv()

    far_first = sorted(range(1, experts), key=lambda by: (abs(by - experts // 2), -by))

    def chunk_out(m, by):
        e = peer("expert", by)
        return remote(
            send.at[m, e], recv[m].at[me_e], disp_send.at[m], disp_recv.at[m], {"expert": e}
        )

    def chunk_self(m):
        return pltpu.make_async_copy(send.at[m, me_e], recv[m].at[me_e], disp_self.at[m])

    def chunks_far(m):
        return remote(
            send.at[m, pl.ds(0, experts - 1)], recv[m].at[pl.ds(0, experts - 1)],
            disp_send.at[m], disp_recv.at[m], {"expert": peer("expert", 1)},
        )

    def back_on(m, by):
        e = peer("expert", by)
        return remote(
            ret_send.at[m, e], ret_recv.at[0, m, me_e], back_send.at[m], back_recv.at[0, m],
            {"expert": e, "section": peer("section", 1)},
        )

    def back_on_all(m):
        return remote(
            ret_send.at[m], ret_recv.at[0, m], back_send.at[m], back_recv.at[0, m],
            {"section": peer("section", 1)},
        )

    def back_home(m, by):
        e = peer("expert", by)
        return remote(
            ret_send.at[m, e], ret_recv.at[1, m, me_e], back_send.at[m], back_recv.at[1, m],
            {"expert": e},
        )

    def back_far(m):
        return remote(
            ret_send.at[m, pl.ds(0, experts - 1)], ret_recv.at[1, m, pl.ds(0, experts - 1)],
            back_send.at[m], back_recv.at[1, m], {"expert": peer("expert", 1)},
        )

    def back_own(m):
        return pltpu.make_async_copy(
            ret_send.at[m, me_e], ret_recv.at[1, m, me_e], back_self.at[m]
        )

    wide = 2 - blocks % 2

    def lanes(i):
        return pl.ds(pl.multiple_of(i * wide * blk, wide * blk), wide * blk)

    def tail_line(e, j):
        return pl.ds(e * tail + j, blocks, stride=tails_all)

    def tail_part(j):
        return pl.ds(blocks + j * folds, folds)

    def put(dst, r, values):
        for e in range(experts):
            dst(e)[r] = values[e * main:(e + 1) * main].astype(BF16)
        tails_by[r] = values[experts * main:]

    def spread_tails(dst, e):
        for j in range(tail):
            lines = tails[tail_line(e, j), :].astype(BF16)
            dst(e)[tail_part(j)] = lines.reshape(folds, main, blk)

    def collect_tails(src):
        for e in range(experts):
            for j in range(tail):
                lines = src(e)[tail_part(j)].reshape(blocks, blk)
                tails[tail_line(e, j), :] = lines.astype(F32)

    def take(src, r):
        pieces_of = [src(e)[r] for e in range(experts)]
        return jnp.concatenate(pieces_of + [tails_by[r].astype(BF16)], axis=0)

    def dispatch(m):
        values = held[m].astype(F32)
        scale = lax.rsqrt(jnp.mean(values * values, axis=-1, keepdims=True) + EPS)
        normed[...] = (values * scale * gain[...]).astype(BF16)

        @pl.loop(0, blocks // wide, unroll=True)
        def _(i):
            values = jnp.dot(disp[m], normed[:, lanes(i)], preferred_element_type=F32)
            for j in range(wide):
                put(lambda e: send.at[m, e], i * wide + j, values[:, j * blk:(j + 1) * blk])

        for e in range(experts):
            spread_tails(lambda e: send.at[m, e], e)

    def send_chunks(m):
        for by in far_first:
            chunk_out(m, by).start()
        chunk_self(m).start()

    def listed(k):
        if k == len(cuts):
            return [
                (group * half + keep + u, groups * keep + group * extra + u)
                for group in range(groups) for u in range(extra)
            ]
        start, size = cuts[k]
        return [
            (group * half + start + u, groups * start + group * size + u)
            for group in range(groups) for u in range(size)
        ]

    whole = [item for k in range(pieces_in) for item in listed(k)]

    def segments(m, s, items):
        for i in range(0, len(items), RUN):
            segment(m, s, items[i:i + RUN])

    def segment(m, s, items):
        products = []
        for c, at in items:
            x = take(lambda e: recv[m].at[e], meta_s[s, 0, c])
            both = jnp.concatenate([weights[0, s, c], weights[1, s, c]], axis=1)
            both = jnp.dot(x, both, preferred_element_type=F32)
            gate, up = both[:, :blk], both[:, blk:]
            hidden = (gate / (1.0 + jnp.exp(-gate)) * up).astype(BF16)
            product = jnp.dot(hidden, weights[2, s, c], preferred_element_type=F32)
            products.append((at, c, product))
        for at, c, product in products:
            parts[s, at] = product + parts[s, meta_s[s, 1, c]]

    def expert_part(m, opening):
        chunk_self(m).wait()
        chunks_far(m).wait()
        collect_tails(lambda e: recv[m].at[e])
        if opening:
            for by in range(1, shards):
                meta_over_shard(by).wait()
            meta_own.wait()
            load = pltpu.make_async_copy(meta_v, meta_s, meta_copy_sem)
            load.start()
            load.wait()
            @pl.when(first)
            def _():
                segments(m, me_s, whole)
                for k in range(pieces_in):
                    finish_stage(k)
                    if k == pieces_in - 1:
                        signal(go_sem, {"section": peer("section", 1)})

                    @pl.loop(1, shards)
                    def _(by):
                        segments(m, peer("shard", shards - by), listed(k))

            @pl.when(me_l > 0)
            def _():
                for k in range(pieces_in):
                    finish_relay(k)

                @pl.loop(0, shards)
                def _(s):
                    segments(m, s, whole)
        else:
            @pl.loop(0, shards)
            def _(s):
                segments(m, s, whole)

        @pl.loop(0, blocks, unroll=True)
        def _(j):
            total = parts[0, meta_s[0, 2, j]]
            for s in range(1, shards):
                total = total + parts[s, meta_s[s, 2, j]]
            put(lambda e: ret_send.at[m, e], j, total)

        for e in range(experts):
            spread_tails(lambda e: ret_send.at[m, e], e)

        @pl.when(me_l < sections - 1)
        def _():
            for by in far_first + [0]:
                back_on(m, by).start()

        @pl.when(last)
        def _():
            for by in far_first:
                back_home(m, by).start()
            back_own(m).start()

    def combine(m, which, dst):
        collect_tails(lambda e: ret_recv.at[which, m, e])

        @pl.loop(0, blocks // wide, unroll=True)
        def _(i):
            values = jnp.concatenate(
                [take(lambda e: ret_recv.at[which, m, e], i * wide + j) for j in range(wide)],
                axis=1,
            )
            mixed = jnp.dot(pieces[which, m], values, preferred_element_type=F32)
            mixed = mixed[:rows] + mixed[rows:2 * rows] + mixed[2 * rows:]
            dst[m, :, lanes(i)] = (held[m, :, lanes(i)].astype(F32) + mixed).astype(BF16)

    def split(which, m, value):
        for i in range(3):
            piece = value.astype(BF16)
            pieces[which, m, i * rows:(i + 1) * rows, :] = piece
            value = value - piece.astype(F32)

    def arrival(c):
        group = sum((c >= g * half).astype(jnp.int32) for g in range(1, groups))
        within = c - group * half
        start = sum(
            (within >= cuts[k][0]).astype(jnp.int32) * cuts[k - 1][1] for k in range(1, len(cuts))
        )
        size = cuts[0][1] + sum(
            (within >= cuts[k][0]).astype(jnp.int32) * (cuts[k][1] - cuts[k - 1][1])
            for k in range(1, len(cuts))
        )
        early = (groups - 1) * start + group * size + within
        return jnp.where(within < keep, early, groups * keep + group * extra + within - keep)

    def iota(shape, axis):
        return lax.broadcasted_iota(jnp.int32, shape, axis)

    slot = iota((slots, rows), 0)
    inner = slot - experts * main
    head = inner < 0
    expert_main = sum((slot >= e * main).astype(jnp.int32) for e in range(1, experts))
    expert_tail = sum((inner >= e * tail).astype(jnp.int32) for e in range(1, experts + 1))
    expert = jnp.where(head, expert_main, expert_tail)
    place_in = jnp.where(head, slot - expert_main * main, main + inner - expert_tail * tail)
    place_in = place_in.astype(F32)
    earlier = (iota((rows, rows), 0) < iota((rows, rows), 1)).astype(F32).astype(BF16)
    for m in range(micro):
        named = [ids[m, j:j + 1, :] == expert for j in range(TOP)]
        hit = functools.reduce(jnp.logical_or, named)
        ahead = jnp.dot(
            hit.astype(F32).astype(BF16), earlier, preferred_element_type=F32
        )
        fits = hit & (ahead == place_in)
        amount = sum(jnp.where(named[j], mix[m, j:j + 1, :], 0.0) for j in range(TOP))
        disp[m] = fits.astype(F32).astype(BF16)
        comb[m] = jnp.transpose(jnp.where(fits, amount, 0.0))

    cols = cols_in[...]
    cols_down = jnp.transpose(jnp.broadcast_to(cols, (n_blk, n_blk)))
    from_place = arrival(iota((n_blk, n_blk), 0))
    chained = (cols_down == cols) & (from_place < arrival(iota((n_blk, n_blk), 1)))
    before = jnp.max(jnp.where(chained, from_place, -1), axis=0, keepdims=True)
    final = jnp.broadcast_to(cols_down[:, :1], (n_blk, blocks)) == iota((n_blk, blocks), 1)
    last_at = jnp.where(final, arrival(iota((n_blk, blocks), 0)), -1)
    last_at = jnp.max(last_at, axis=0, keepdims=True)
    meta_here[...] = jnp.zeros_like(meta_here)
    meta_here[0:1, 0:n_blk] = rows_in[...]
    meta_here[1:2, 0:n_blk] = jnp.where(before < 0, n_blk, before)
    meta_here[2:3, 0:blocks] = jnp.where(last_at < 0, n_blk, last_at)
    for s in range(shards):
        parts[s, n_blk] = jnp.zeros_like(parts[s, n_blk])

    for m in range(micro):
        token_copy(m).wait()

    @pl.when(first)
    def _():
        dispatch(0)

    @pl.when(last)
    def _():
        for m in range(micro):
            split(1, m, comb[m])

    mine = weights.at[:, me_s]
    pltpu.make_async_copy(mine, mine, own_sem).wait()
    pl.semaphore_wait(barrier, greeted)

    for by in range(1, shards):
        meta_over_shard(by).start()
    meta_own.start()

    @pl.when(first)
    def _():
        start_stage()
        send_chunks(0)

    @pl.when(me_l < sections - 1)
    def _():
        comb_copy().start()

    @pl.when(first)
    def _():
        for m in range(1, micro):
            dispatch(m)
            send_chunks(m)

    @pl.when(me_l > 0)
    def _():
        for k, by in relayed:
            stage_in(k, by).wait_recv()
            for hop in range(1, groups):
                stage_over(k, by, hop, me_g).start()
            start_down(k, by)
        comb_copy().wait_recv()
        for m in range(micro):
            split(0, m, comb_in[m])
        pl.semaphore_wait(go_sem, 1)
        start_weights()
        early = max(0, pieces_in - 5)
        for m in range(micro):
            if m == 0:
                relay_weights(0, early)
            back_on_all(m).wait_recv()
            if m > 0:
                send_chunks(m - 1)
            combine(m, 0, held)
            hand_back(m).start()
            dispatch(m)
        send_chunks(micro - 1)
        relay_weights(early, pieces_in)

    for m in range(micro):
        expert_part(m, m == 0)

    @pl.when(last)
    def _():
        for m in range(micro):
            back_own(m).wait()
            back_far(m).wait()
            combine(m, 1, out)

    @pl.when(me_l > 0)
    def _():
        for m in range(micro):
            hand_back(m).wait_send()
        all_sent(wx_send)
        all_sent(sc_send, keep)
        for hop in range(1, groups):
            all_sent(sy_send.at[hop - 1], keep)
            all_sent(wy_send.at[hop - 1], keep)

    @pl.when(me_l < sections - 1)
    def _():
        comb_copy().wait_send()
        all_sent(sx_send)
        for m in range(micro):
            back_on_all(m).wait_send()
            hand_back(m).wait_recv()


def body(
    sizes,
    tokens,
    norm_gain,
    route_ids,
    route_weights,
    gate_blocks,
    up_blocks,
    down_blocks,
    gate_rows,
    down_cols,
):
    groups, shards, experts, sections = sizes
    assert sections == 2
    micro, rows, width = tokens.shape
    n_blk, blk = gate_blocks.shape[2], gate_blocks.shape[-1]
    blocks = width // blk
    cap = min(rows, max(rows * 9 // 16, rows * TOP // experts + 2))
    main = cap // 16 * 16
    tails_all = -(-(experts * (cap - main)) // 8) * 8
    slots = experts * main + tails_all

    extra = both_ways(n_blk // groups, groups)
    keep = n_blk // groups - extra
    cuts = len(cut_list(keep)) + min(extra, 1)
    meta_width = -(-max(n_blk, blocks) // 128) * 128
    dims = (micro, rows, blocks, blk, cap, experts, shards, groups, sections, n_blk)
    dma = pltpu.SemaphoreType.DMA
    assert blocks % main == 0
    chunk = (micro, experts, cap * blocks // main, main, blk)
    vmem, anywhere = pl.BlockSpec(memory_space=pltpu.VMEM), pl.BlockSpec(memory_space=pltpu.HBM)
    out = pl.pallas_call(
        functools.partial(layer_kernel, dims),
        out_shape=pltpu.VMEM((micro, rows, width), BF16),
        in_specs=[anywhere] + [vmem] * 3 + [anywhere] * 3 + [vmem] * 2,
        out_specs=vmem,
        scratch_shapes=[
            pltpu.VMEM((micro, rows, width), BF16),
            pltpu.VMEM((micro, slots, rows), BF16),
            pltpu.VMEM((micro, rows, slots), F32),
            pltpu.VMEM((micro, rows, slots), F32),
            pltpu.VMEM((2, micro, 3 * rows, slots), BF16),
            pltpu.VMEM((8, meta_width), jnp.int32),
            pltpu.VMEM((rows, width), BF16),
            pltpu.VMEM((tails_all * blocks, blk), F32),
            pltpu.VMEM(chunk, BF16),
            [pltpu.VMEM(chunk[1:], BF16) for _ in range(micro)],
            pltpu.VMEM((shards, n_blk + 1, slots, blk), F32),
            pltpu.VMEM(chunk, BF16),
            pltpu.VMEM((2,) + chunk, BF16),
            pltpu.VMEM((3, shards, n_blk, blk, blk), BF16),
            pltpu.VMEM((3, shards, keep + groups * extra, blk, blk), BF16),
            pltpu.VMEM((shards, 8, meta_width), jnp.int32),
            pltpu.SMEM((shards, 8, meta_width), jnp.int32),
            dma((micro,)),
            dma((2, micro)),
            dma,
            dma,
            dma((shards - 1,)),
            dma((shards - 1,)),
            dma,
            dma((2,)),
            dma,
            dma((cuts, shards - 1)),
            dma((groups - 1,)),
            dma((cuts, shards - 1, groups - 1)),
            dma((micro,)),
            dma((micro,)),
            dma((micro,)),
            dma((micro,)),
            dma((2, micro)),
            dma((micro,)),
            dma,
            dma((cuts, shards - 1)),
            dma,
            dma((groups - 1,)),
            pltpu.SemaphoreType.REGULAR,
        ],
        compiler_params=pltpu.CompilerParams(
            collective_id=0, has_side_effects=True, vmem_limit_bytes=56 * 1024 * 1024
        ),
    )(
        tokens, norm_gain, jnp.swapaxes(route_ids[0], 1, 2), jnp.swapaxes(route_weights[0], 1, 2),
        gate_blocks.reshape(n_blk, blk, blk), up_blocks.reshape(n_blk, blk, blk),
        down_blocks.reshape(n_blk, blk, blk), gate_rows.reshape(1, n_blk),
        down_cols.reshape(1, n_blk),
    )
    return out[None]


def solution(mesh):
    sizes = tuple(mesh.shape[name] for name in ("groups", "shard", "expert", "section"))
    in_specs = (
        P(None, ("groups", "shard", "expert"), None),
        P("section", None),
        P("section", None, ("groups", "shard", "expert"), None),
        P("section", None, ("groups", "shard", "expert"), None),
        P("section", "expert", "shard", None, None, None),
        P("section", "expert", "shard", None, None, None),
        P("section", "expert", "shard", None, None, None),
        P("section", "expert", "shard", None),
        P("section", "expert", "shard", None),
    )
    out_specs = P("section", None, ("groups", "shard", "expert"), None)
    return jax.shard_map(
        functools.partial(body, sizes), mesh=mesh, in_specs=in_specs, out_specs=out_specs,
        check_vma=False,
    )
```
